32 devices in a mesh: row: 8 (over y, x, core), col: 4 (over z).
Axes of the slice: x: 2, y: 2, z: 4, core: 2. Of those that a mesh axis runs over, the one named last changes fastest.
Arguments:
- inputs: bfloat16 [4096, 2048], P('col', 'row'), may hold values from -6 to 6
- cotangent: bfloat16 [4096, 2048], P('col', 'row'), may hold values from -6 to 6
- seq_blocks: int32 [4], replicated, may hold values from 1 to 12, 16 in all
- first_gain: float32 [2048], P('row'), may hold values from 0.5 to 1.5
- first_shift: float32 [2048], P('row'), may hold values from -1.75 to 1.75
- w_query: bfloat16 [2048, 2048], P('row', 'col'), may hold values from -0.125 to 0.125
- b_query: float32 [2048], P('col'), may hold values from -3 to 3
- w_keyval: bfloat16 [2048, 256], P('row', 'col'), may hold values from -0.125 to 0.125
- b_value: float32 [128], replicated, may hold values from -0.3125 to 0.3125
- w_out: bfloat16 [2048, 2048], P('col', 'row'), may hold values from -2 to 2
- b_out: float32 [2048], P('row'), may hold values from -3 to 3
- second_gain: float32 [2048], P('row'), may hold values from 0.5 to 1.5
- second_shift: float32 [2048], P('row'), may hold values from -1.75 to 1.75
- w_up: bfloat16 [2048, 8192], P('row', 'col'), may hold values from -0.125 to 0.125
- b_up: float32 [8192], P('col'), may hold values from -3 to 3
- w_down: bfloat16 [8192, 2048], P('col', 'row'), may hold values from -0.125 to 0.125
- b_down: float32 [2048], P('row'), may hold values from -3 to 3
Outputs:
- block_output: bfloat16 [4096, 2048], P('col', 'row')
- grad_inputs: float32 [4096, 2048], P('col', 'row')
- grad_first_gain: float32 [2048], P('row')
- grad_first_shift: float32 [2048], P('row')
- grad_w_query: float32 [2048, 2048], P('row', 'col')
- grad_b_query: float32 [2048], P('col')
- grad_w_keyval: float32 [2048, 256], P('row', 'col')
- grad_b_value: float32 [128], replicated
- grad_w_out: float32 [2048, 2048], P('col', 'row')
- grad_b_out: float32 [2048], P('row')
- grad_second_gain: float32 [2048], P('row')
- grad_second_shift: float32 [2048], P('row')
- grad_w_up: float32 [2048, 8192], P('row', 'col')
- grad_b_up: float32 [8192], P('col')
- grad_w_down: float32 [8192, 2048], P('col', 'row')
- grad_b_down: float32 [2048], P('row')
The draws below stay inside these ranges and needn't reach their ends.
Inputs may be any that keep to these rules, and one draw needn't show every extreme that they name: seq_blocks sums to 16, and its largest entry is exactly 12.
All inputs are finite; a program needn't handle non-finite values.
Results may differ from the reference program's by a relative error of at most 0.033.
Values may be sent and summed in bfloat16 or wider, within the bound.
No kernel may reach another device: no remote copies, remote signals or barrier semaphores. Data moves between devices by JAX's collectives and lax.ppermute only.
A program may use at most 320 MiB of HBM per device.

```python
import math
import jax
import jax.numpy as jnp
import numpy as np
from jax import lax

D = 2048
HEADS = 16
HD = 128
F = 8192
BLK = 256
BQ = 512
TOKENS = 4096
NBLK = 16
NSEQ = 4
SEQ_MOST = 12


def block_scale(key, extent, split, smallest, top_value):
    def one(axis_at, parts):
        heights = jax.random.uniform(jax.random.fold_in(jax.random.fold_in(key, 6), axis_at), (parts,), jnp.float32, smallest / len(split), top_value / len(split))
        return jnp.repeat(jnp.exp(heights), extent[axis_at] // parts).reshape((-1,) + (1,) * (len(extent) - axis_at - 1))

    factor_of = one(*split[0])
    for cut in split[1:]:
        factor_of = factor_of * one(*cut)
    return factor_of


def profile(count, total, most, skew):
    loads = [(1 << 20) // math.isqrt(rank ** skew) + 1 for rank in range(2, count + 1)]
    spare, given = total - most - (count - 1), [1] * (count - 1)
    while spare > 0:
        movable = [i for i in range(count - 1) if given[i] < most]
        pool, left = sum([loads[i] for i in movable]), spare
        for i in movable:
            more = min(most - given[i], max(1, left * loads[i] // pool), spare)
            given[i] = given[i] + more
            spare = spare - more
    return np.array([most] + given)


def uneven_parts(stream_key, amount, total, bound, lean):
    if amount == 2:
        one = jax.random.randint(stream_key, (), max(1, total - bound), min(bound, total - 1) + 1)
        return jnp.stack([one, total - one])
    lengths = jnp.asarray(profile(amount, total, bound, lean), jnp.int32)
    couples = (amount - 1) // 2
    donor, taker = lengths[1:1 + 2 * couples:2], lengths[2:2 + 2 * couples:2]
    margin = jnp.minimum(donor - 1, bound - taker)
    moved = jax.random.randint(jax.random.fold_in(stream_key, 1), (couples,), 0, 1 << 20) % (margin + 1)
    lengths = lengths.at[1:1 + 2 * couples:2].set(donor - moved).at[2:2 + 2 * couples:2].set(taker + moved)
    return lengths[jax.random.permutation(jax.random.fold_in(stream_key, 2), amount)]


def noise(stream_key, shape, width, reach, cuts=(), kind=jnp.bfloat16):
    array = jax.random.normal(stream_key, shape, jnp.float32) * width
    if len(cuts) > 0:
        array = block_scale(stream_key, shape, cuts, -0.22, 0.18) * array
    return jnp.clip(array, min=-reach, max=reach).astype(kind)


def setup_inputs(seed: int = 0) -> dict:
    splits = jax.random.split(jax.random.key(seed), 18)
    inputs = noise(splits[0], (TOKENS, D), 1.0, 6.0, ((0, 4), (1, 8)))
    cotangent = noise(splits[1], (TOKENS, D), 1.0, 6.0, ((0, 4), (1, 8)))
    seq_blocks = uneven_parts(splits[2], NSEQ, NBLK, SEQ_MOST, 1).astype(jnp.int32)
    first_gain = jnp.clip(1.0 + 0.1 * jax.random.normal(splits[3], (D,), jnp.float32), 0.5, 1.5)
    first_shift = noise(splits[4], (D,), 0.3, 1.75, ((0, 8),), jnp.float32)
    w_query = noise(splits[5], (D, D), D ** -0.5, 0.125, ((0, 8), (1, 4)))
    b_query = noise(splits[6], (D,), 0.5, 3.0, ((0, 4),), jnp.float32)
    w_keyval = noise(splits[7], (D, 2 * HD), D ** -0.5, 0.125, ((0, 8), (1, 4)))
    b_value = noise(splits[8], (HD,), 0.05, 0.3125, (), jnp.float32)
    w_out = noise(splits[9], (D, D), (max(4, D // 256)) ** -0.5, 2.0, ((0, 4), (1, 8)))
    b_out = noise(splits[10], (D,), 0.5, 3.0, ((0, 8),), jnp.float32)
    second_gain = jnp.clip(1.0 + 0.1 * jax.random.normal(splits[11], (D,), jnp.float32), 0.5, 1.5)
    second_shift = noise(splits[12], (D,), 0.3, 1.75, ((0, 8),), jnp.float32)
    w_up = noise(splits[13], (D, F), D ** -0.5, 0.125, ((0, 8), (1, 4)))
    b_up = noise(splits[14], (F,), 0.5, 3.0, ((0, 4),), jnp.float32)
    w_down = noise(splits[15], (F, D), (F // 4) ** -0.5, 0.125, ((0, 4), (1, 8)))
    b_down = noise(splits[16], (D,), 0.5, 3.0, ((0, 8),), jnp.float32)
    return {"inputs": inputs, "cotangent": cotangent, "seq_blocks": seq_blocks, "first_gain": first_gain, "first_shift": first_shift, "w_query": w_query, "b_query": b_query, "w_keyval": w_keyval, "b_value": b_value, "w_out": w_out, "b_out": b_out, "second_gain": second_gain, "second_shift": second_shift, "w_up": w_up, "b_up": b_up, "w_down": w_down, "b_down": b_down}


EPSILON = 1e-05
NEGATIVE = -1e+30

@jax.custom_vjp
def low(v):
    return lax.optimization_barrier(v.astype(jnp.bfloat16)).astype(jnp.float32)

@jax.custom_vjp
def low_back(v):
    return v

def low_keep(v):
    return (low(v), None)

def low_pass(kept, grad):
    return (grad,)

def back_keep(v):
    return (v, None)

def back_low(kept, grad):
    return (low(grad),)
low.defvjp(low_keep, low_pass)
low_back.defvjp(back_keep, back_low)

def matmul(left, right):
    return jnp.dot(left, right, precision=lax.Precision.HIGHEST)

def layer_norm(values, gain, shift):
    mean = lax.optimization_barrier(jnp.mean(values, 1, keepdims=True))
    centred = values - mean
    variance = lax.optimization_barrier(jnp.mean(centred * centred, 1, keepdims=True))
    return centred * lax.rsqrt(variance + EPSILON) * gain + shift

def attention_core(queries, keyval, seq_blocks):
    positions = jnp.arange(TOKENS, dtype=jnp.int32)
    ends = (jnp.cumsum(seq_blocks) * BLK).astype(jnp.int32)
    owners = lax.optimization_barrier(jnp.sum((positions[:, None] >= ends[None, :]).astype(jnp.int32), 1)).astype(jnp.int32)
    blocks = (positions // BLK).astype(jnp.int32)
    query_rows = min(BQ, TOKENS)
    window = min(TOKENS, SEQ_MOST * BLK + query_rows)
    scale = HD ** (-0.5)

    def one_block(index):
        query_first = (index * query_rows).astype(jnp.int32)
        key_first = jnp.clip(query_first + query_rows - window, 0, TOKENS - window).astype(jnp.int32)
        block_query = lax.dynamic_slice_in_dim(queries, query_first, query_rows, 0).reshape(query_rows, HEADS, HD)
        block_kv = lax.dynamic_slice_in_dim(keyval, key_first, window, 0)
        query_owner = lax.dynamic_slice_in_dim(owners, query_first, query_rows, 0)
        key_owner = lax.dynamic_slice_in_dim(owners, key_first, window, 0)
        query_block = lax.dynamic_slice_in_dim(blocks, query_first, query_rows, 0)
        key_block = lax.dynamic_slice_in_dim(blocks, key_first, window, 0)
        allowed = (query_owner[:, None] == key_owner[None, :]) & (key_block[None, :] <= query_block[:, None])
        scores = low_back(jnp.einsum('qhd,kd->hqk', block_query, block_kv[:, :HD], precision=lax.Precision.HIGHEST) * scale)
        scores = jnp.where(allowed[None], scores, NEGATIVE)
        largest = lax.optimization_barrier(jnp.max(scores, 2, keepdims=True))
        expd = jnp.where(allowed[None], jnp.exp(scores - largest), 0.0)
        probs = low(expd / lax.optimization_barrier(jnp.sum(expd, 2, keepdims=True)))
        output = jnp.einsum('hqk,kd->qhd', probs, block_kv[:, HD:], precision=lax.Precision.HIGHEST)
        return output.reshape(query_rows, HEADS * HD)
    outputs = lax.map(jax.checkpoint(one_block), jnp.arange(TOKENS // query_rows, dtype=jnp.int32))
    return outputs.reshape(TOKENS, HEADS * HD)

def forward(inputs, first_gain, first_shift, w_query, b_query, w_keyval, b_value, w_out, b_out, second_gain, second_shift, w_up, b_up, w_down, b_down, seq_blocks):
    first_in = low(layer_norm(inputs, first_gain, first_shift))
    queries = low(low_back(matmul(first_in, w_query) + b_query))
    keyval = low(low_back(matmul(first_in, w_keyval)))
    core = attention_core(queries, keyval, seq_blocks)
    attn_in = low(low_back(core + jnp.tile(b_value, HEADS)))
    middle = inputs + low_back(matmul(attn_in, w_out) + b_out)
    second_in = low(layer_norm(middle, second_gain, second_shift))
    pre = low_back(matmul(second_in, w_up) + b_up)
    hidden = low(jax.nn.gelu(pre, approximate=True))
    return middle + low_back(matmul(hidden, w_down) + b_down)

def reference(inputs, cotangent, seq_blocks, first_gain, first_shift, w_query, b_query, w_keyval, b_value, w_out, b_out, second_gain, second_shift, w_up, b_up, w_down, b_down):
    floats = tuple((value.astype(jnp.float32) for value in (inputs, first_gain, first_shift, w_query, b_query, w_keyval, b_value, w_out, b_out, second_gain, second_shift, w_up, b_up, w_down, b_down)))

    def wrapped(*values):
        return forward(*values, seq_blocks)
    output, pullback = jax.vjp(wrapped, *floats)
    grads = pullback(cotangent.astype(jnp.float32))
    return (output.astype(jnp.bfloat16), grads[0], grads[1], grads[2], grads[3], grads[4], grads[5], grads[6], grads[7], grads[8], grads[9], grads[10], grads[11], grads[12], grads[13], grads[14])
```

```python
from functools import partial

import jax
import jax.numpy as jnp
from jax import lax
from jax.experimental import pallas as pl
from jax.experimental.pallas import tpu as pltpu
from jax.sharding import PartitionSpec as P

BLK = 256
EPSILON = 1e-05
NEGATIVE = -1e30
LOG2E = 1.4426950408889634
F32 = jnp.float32
BF16 = jnp.bfloat16


def barrier(*values):
    return lax.optimization_barrier(values)


def col_parts(value):
    count = lax.axis_size("col")
    return [
        lax.ppermute(value, "col", [(i, (i + step) % count) for i in range(count)])
        for step in range(1, count)
    ]


def col_join(value, parts):
    count = lax.axis_size("col")
    me = lax.axis_index("col")
    out = jnp.zeros((count,) + value.shape, value.dtype)
    out = lax.dynamic_update_index_in_dim(out, value, me, 0)
    for step, part in enumerate(parts, 1):
        out = lax.dynamic_update_index_in_dim(out, part, lax.rem(me - step + count, count), 0)
    return out


def col_send(pieces):
    count = lax.axis_size("col")
    me = lax.axis_index("col")
    low = pieces.astype(BF16)
    out = [lax.dynamic_index_in_dim(low, me, 0, keepdims=False)]
    for step in range(1, count):
        part = lax.dynamic_index_in_dim(low, lax.rem(me + step, count), 0, keepdims=False)
        out.append(
            lax.ppermute(part, "col", [(i, (i + step) % count) for i in range(count)])
        )
    return out


def add_up(parts):
    return sum(part.astype(F32) for part in parts)


def exchange_rows(pieces):
    return lax.all_to_all(pieces.astype(BF16), "row", 0, 0)


def total(pieces):
    return jnp.sum(pieces.astype(F32), 0)


def swap(value, bit):
    count = lax.axis_size("row")
    return lax.ppermute(value, "row", [(i, i ^ bit) for i in range(count)])


def chip_bits():
    bits = []
    bit = 2
    while bit < lax.axis_size("row"):
        bits.append(bit)
        bit *= 2
    return bits


def row_place(other):
    apart = jnp.bitwise_xor(lax.axis_index("row"), other)
    return (apart & 1) * (lax.axis_size("row") // 2) + (apart >> 1)


def in_row_order(pieces, axis):
    count = pieces.shape[0]
    return jnp.concatenate(
        [
            lax.dynamic_index_in_dim(pieces, row_place(a), 0, keepdims=False)
            for a in range(count)
        ],
        axis,
    )


def row_gather(value):
    half = value.shape[-1] // 2
    bits = chip_bits()
    orders = (bits, bits[::-1])
    held = [{0: value[..., :half]}, {0: value[..., half:]}]
    for step in range(len(bits)):
        keys = [sorted(h) for h in held]
        got = yield [
            swap(jnp.stack([h[k] for k in ks]), order[step])
            for h, ks, order in zip(held, keys, orders)
        ]
        for h, ks, order, new in zip(held, keys, orders, got):
            h.update({k ^ order[step]: new[n] for n, k in enumerate(ks)})
    own = jnp.stack([jnp.concatenate([held[0][k], held[1][k]], -1) for k in sorted(held[0])])
    (other,) = yield [swap(own, 1)]
    return own, other


def row_scatter(mine, theirs):
    got = yield [swap(part, 1) for part in theirs]
    bits = chip_bits()
    orders = (bits[::-1], bits)
    held = []
    for part, new in zip(mine, got):
        both = part + new.astype(F32)
        held.append({2 * k: both[k] for k in range(both.shape[0])})
    for step in range(len(bits)):
        keeps = [sorted(k for k in h if not k & order[step]) for h, order in zip(held, orders)]
        got = yield [
            swap(jnp.stack([h[k ^ order[step]] for k in keep]).astype(BF16), order[step])
            for h, keep, order in zip(held, keeps, orders)
        ]
        held = [
            {k: h[k] + new[n].astype(F32) for n, k in enumerate(keep)}
            for h, keep, new in zip(held, keeps, got)
        ]
    return [h[0] for h in held]


def advance(steps, arrived):
    try:
        return steps.send(list(arrived))
    except StopIteration as stop:
        return {"done": stop.value}


def finish(steps, arrived):
    while True:
        arrived = advance(steps, list(barrier(*arrived)))
        if isinstance(arrived, dict):
            return arrived["done"]


def in_parts(vector, count):
    parts = []
    for _ in range(count):
        low = lax.reduce_precision(vector, 8, 7)
        parts.append(low.astype(BF16))
        vector = vector - low
    return jnp.stack(parts)


def padded(rows_array, multiple):
    short = -rows_array.shape[0] % multiple
    return jnp.pad(rows_array, ((0, short), (0, 0)))


def norm_kernel(
    me_ref, mine_ref, theirs_ref, mine_vec, theirs_vec, mine_own, theirs_own,
    first_ref, own_ref, vector_ref,
    *, width
):
    half = mine_ref.shape[0]
    features = mine_ref.shape[2]
    places = [(mine_ref, mine_vec, mine_own, 2 * k, k) for k in range(half)]
    places += [(theirs_ref, theirs_vec, theirs_own, 2 * k + 1, k) for k in range(half)]
    me = me_ref[0]

    def columns(apart):
        return pl.ds(pl.multiple_of(jnp.bitwise_xor(me, apart) * features, features), features)

    @pl.when(pl.program_id(0) == 0)
    def _():
        for _, vec, own, apart, k in places:
            stack = vec[k].astype(F32)
            vector_ref[:, columns(apart)] = stack[0:8] + stack[8:16] + stack[16:24]
            own_ref[:, columns(apart)] = own[k]

    sums = sum(jnp.sum(ref[k].astype(F32), 1, keepdims=True) for ref, _, _, _, k in places)
    mean = sums / width
    squares = jnp.zeros_like(mean)
    for ref, _, _, _, k in places:
        centred = ref[k].astype(F32) - mean
        squares = squares + jnp.sum(centred * centred, 1, keepdims=True)
    scale = lax.rsqrt(squares / width + EPSILON)
    for ref, vec, _, apart, k in places:
        stack = vec[k].astype(F32)
        both = stack[0:8] + stack[8:16] + stack[16:24]
        normed = (ref[k].astype(F32) - mean) * scale
        first_ref[:, columns(apart)] = (normed * both[0:1] + both[1:2]).astype(BF16)


def norm_gathered(mine, theirs, tokens, span):
    rows = lax.axis_size("row")
    half, _, features = mine.shape
    width = features * rows
    me = jnp.full((1,), lax.axis_index("row"), jnp.int32)
    block = pl.BlockSpec((half, BLK, features), lambda i, _: (0, i, 0))
    vec = pl.BlockSpec((half, 32, features), lambda i, _: (0, tokens // 32, 0))
    own = pl.BlockSpec((half, span, features), lambda i, m: (0, m[0], 0))
    return pl.pallas_call(
        partial(norm_kernel, width=width),
        out_shape=(
            jax.ShapeDtypeStruct((tokens, width), BF16),
            jax.ShapeDtypeStruct((span, width), BF16),
            jax.ShapeDtypeStruct((8, width), F32),
        ),
        grid_spec=pltpu.PrefetchScalarGridSpec(
            num_scalar_prefetch=1,
            grid=(tokens // BLK,),
            in_specs=[block, block, vec, vec, own, own],
            out_specs=(
                pl.BlockSpec((BLK, width), lambda i, _: (i, 0)),
                pl.BlockSpec((span, width), lambda i, _: (0, 0)),
                pl.BlockSpec((8, width), lambda i, _: (0, 0)),
            ),
        ),
        name="norm_gathered",
    )(me, mine, theirs, mine, theirs, mine, theirs)


def stacked_heads(block, head_dim):
    count = block.shape[1] // head_dim
    return jnp.concatenate([block[:, h * head_dim : (h + 1) * head_dim] for h in range(count)], 0)


def dot_last(left, right):
    return lax.dot_general(left, right, (((1,), (1,)), ((), ())), preferred_element_type=F32)


def dot_first(left, right):
    return lax.dot_general(left, right, (((0,), (0,)), ((), ())), preferred_element_type=F32)


def dot_plain(left, right):
    return lax.dot_general(left, right, (((1,), (0,)), ((), ())), preferred_element_type=F32)


def key_pieces(kb, me, per_col, per_block, half):
    col = lax.div(kb, per_col)
    first = lax.rem(kb, per_col) * per_block
    places = []
    for t in range(per_block):
        apart = jnp.bitwise_xor(first + t, me)
        places.append((apart & 1) * half + lax.shift_right_logical(apart, 1))
    return col, places


def forward_kernel(
    low_ref, high_ref, me_ref, q_ref, kv_ref, bias_ref, out_ref, log_ref, low_out_ref, acc_ref, top_ref, sum_ref,
    *, head_dim, per_col, per_block, span
):
    chunk = pl.program_id(0)
    q = stacked_heads(q_ref[...], head_dim)
    rows = q.shape[0]
    acc_ref[...] = jnp.zeros_like(acc_ref)
    top_ref[...] = jnp.full_like(top_ref, NEGATIVE)
    sum_ref[...] = jnp.zeros_like(sum_ref)
    factor = head_dim ** (-0.5) * LOG2E

    def visit(kb, carry):
        col, places = key_pieces(kb, me_ref[0], per_col, per_block, kv_ref.shape[0] // 2)
        at = pl.ds(pl.multiple_of(col * span, span), span)
        kv = jnp.concatenate([kv_ref[place, at, :] for place in places], 0)
        scores = dot_last(kv[:, :head_dim], q) * factor
        old = top_ref[...]
        new = jnp.maximum(old, jnp.max(scores, 0, keepdims=True))
        weights = jnp.exp2(scores - new)
        decay = jnp.exp2(old - new)
        top_ref[...] = new
        sum_ref[...] = sum_ref[...] * decay + jnp.sum(weights, 0, keepdims=True)
        acc_ref[...] = acc_ref[...] * decay + dot_first(kv[:, head_dim:], weights.astype(BF16))
        return carry

    lax.fori_loop(low_ref[chunk], high_ref[chunk], visit, 0)
    out = acc_ref[...] / sum_ref[...]
    out_ref[0] = out
    for h in range(rows // BLK):
        low_out_ref[:, h * head_dim : (h + 1) * head_dim] = (
            jnp.transpose(out[:, h * BLK : (h + 1) * BLK]) + bias_ref[...]
        ).astype(BF16)
    log_ref[0] = top_ref[...] + jnp.log2(sum_ref[...])


def backward_kernel(
    low_ref, high_ref, me_ref, q_ref, grad_ref, out_ref, log_ref, kv_ref, gq_ref, gk_mine, gk_theirs, gv_mine, gv_theirs,
    gk_acc, gv_acc, gq_acc,
    *, head_dim, per_col, per_block, span
):
    chunk = pl.program_id(0)

    @pl.when(chunk == 0)
    def _():
        gk_acc[...] = jnp.zeros_like(gk_acc)
        gv_acc[...] = jnp.zeros_like(gv_acc)

    q = stacked_heads(q_ref[...], head_dim)
    grad = stacked_heads(grad_ref[...], head_dim)
    scale = head_dim ** (-0.5)
    log = log_ref[0]
    delta = jnp.sum(out_ref[0] * jnp.transpose(grad.astype(F32)), 0, keepdims=True)
    gq_acc[...] = jnp.zeros_like(gq_acc)

    def visit(kb, carry):
        col, places = key_pieces(kb, me_ref[0], per_col, per_block, kv_ref.shape[0] // 2)
        at = pl.ds(pl.multiple_of(col * span, span), span)
        kv = jnp.concatenate([kv_ref[place, at, :] for place in places], 0)
        keys, vals = kv[:, :head_dim], kv[:, head_dim:]
        scores = dot_last(keys, q) * (scale * LOG2E)
        probs = jnp.exp2(scores - log)
        grad_probs = dot_last(vals, grad)
        grad_scores = (probs * (grad_probs - delta)).astype(BF16)
        gq_acc[...] += dot_first(keys, grad_scores)
        gk = dot_plain(grad_scores, q)
        gv = dot_plain(probs.astype(BF16), grad)
        for t, place in enumerate(places):
            gk_acc[place, at, :] += gk[t * span : (t + 1) * span]
            gv_acc[place, at, :] += gv[t * span : (t + 1) * span]
        return carry

    lax.fori_loop(low_ref[chunk], high_ref[chunk], visit, 0)
    gq = gq_acc[...] * scale
    for h in range(q.shape[0] // BLK):
        gq_ref[:, h * head_dim : (h + 1) * head_dim] = jnp.transpose(
            gq[:, h * BLK : (h + 1) * BLK]
        ).astype(BF16)

    @pl.when(chunk == pl.num_programs(0) - 1)
    def _():
        half = gk_mine.shape[0]
        gk_mine[...] = gk_acc[:half] * scale
        gk_theirs[...] = (gk_acc[half:] * scale).astype(BF16)
        gv_mine[...] = gv_acc[:half]
        gv_theirs[...] = gv_acc[half:].astype(BF16)


def attention_calls(seq_blocks, tokens_col, span, head_dim, query_cols):
    rows, cols = lax.axis_size("row"), lax.axis_size("col")
    per_col, per_block = tokens_col // BLK, BLK // span
    heads = query_cols // head_dim
    me = lax.axis_index("row")
    ends = jnp.cumsum(seq_blocks)
    blocks = lax.axis_index("col") * per_col + jnp.arange(per_col, dtype=jnp.int32)
    owner = jnp.sum((blocks[:, None] >= ends[None, :]).astype(jnp.int32), 1)
    starts = ends - seq_blocks
    low = jnp.sum(
        jnp.where(owner[:, None] == jnp.arange(ends.shape[0])[None, :], starts[None, :], 0), 1
    ).astype(jnp.int32)
    scalars = (low, (blocks + 1).astype(jnp.int32), jnp.full((1,), me, jnp.int32))
    sizes = dict(head_dim=head_dim, per_col=per_col, per_block=per_block, span=span)
    chunk_rows = pl.BlockSpec((BLK, query_cols), lambda c, *_: (c, 0))
    whole_kv = pl.BlockSpec((rows, cols * span, 2 * head_dim), lambda c, *_: (0, 0, 0))
    half_kv = pl.BlockSpec((rows // 2, cols * span, head_dim), lambda c, *_: (0, 0, 0))
    turned = pl.BlockSpec((1, head_dim, heads * BLK), lambda c, *_: (c, 0, 0))
    logs = pl.BlockSpec((1, 1, heads * BLK), lambda c, *_: (c, 0, 0))
    bias = pl.BlockSpec((1, head_dim), lambda c, *_: (0, 0))
    shape = jax.ShapeDtypeStruct

    def forward(queries, key_values, bias_value):
        return pl.pallas_call(
            partial(forward_kernel, **sizes),
            out_shape=(
                shape((per_col, head_dim, heads * BLK), F32),
                shape((per_col, 1, heads * BLK), F32),
                shape((tokens_col, query_cols), BF16),
            ),
            grid_spec=pltpu.PrefetchScalarGridSpec(
                num_scalar_prefetch=3,
                grid=(per_col,),
                in_specs=[chunk_rows, whole_kv, bias],
                out_specs=(turned, logs, chunk_rows),
                scratch_shapes=[
                    pltpu.VMEM((head_dim, heads * BLK), F32),
                    pltpu.VMEM((1, heads * BLK), F32),
                    pltpu.VMEM((1, heads * BLK), F32),
                ],
            ),
            name="attend_forward",
        )(*scalars, queries, key_values, bias_value)

    def backward(queries, grad_low, out, log, key_values):
        return pl.pallas_call(
            partial(backward_kernel, **sizes),
            out_shape=(
                shape((tokens_col, query_cols), BF16),
                shape((rows // 2, cols * span, head_dim), F32),
                shape((rows // 2, cols * span, head_dim), BF16),
                shape((rows // 2, cols * span, head_dim), F32),
                shape((rows // 2, cols * span, head_dim), BF16),
            ),
            grid_spec=pltpu.PrefetchScalarGridSpec(
                num_scalar_prefetch=3,
                grid=(per_col,),
                in_specs=[chunk_rows, chunk_rows, turned, logs, whole_kv],
                out_specs=(chunk_rows, half_kv, half_kv, half_kv, half_kv),
                scratch_shapes=[
                    pltpu.VMEM((rows, cols * span, head_dim), F32),
                    pltpu.VMEM((rows, cols * span, head_dim), F32),
                    pltpu.VMEM((head_dim, heads * BLK), F32),
                ],
            ),
            name="attend_backward",
        )(*scalars, queries, grad_low, out, log, key_values)

    return forward, backward


def norm_forward(values):
    mean = jnp.mean(values, 1, keepdims=True)
    centred = values - mean
    scale = lax.rsqrt(jnp.mean(centred * centred, 1, keepdims=True) + EPSILON)
    return centred * scale, scale


def norm_backward(grad_out, normed, scale, gain):
    grad_normed = grad_out * gain
    plain = jnp.mean(grad_normed, 1, keepdims=True)
    cross = jnp.mean(grad_normed * normed, 1, keepdims=True)
    grad_in = scale * (grad_normed - plain - normed * cross)
    return grad_in, jnp.sum(grad_out * normed, 0), jnp.sum(grad_out, 0)


def body(
    inputs,
    cotangent,
    seq_blocks,
    first_gain,
    first_shift,
    w_query,
    b_query,
    w_keyval,
    b_value,
    w_out,
    b_out,
    second_gain,
    second_shift,
    w_up,
    b_up,
    w_down,
    b_down,
):
    rows, cols = lax.axis_size("row"), lax.axis_size("col")
    row, col = lax.axis_index("row"), lax.axis_index("col")
    tokens_col, features = inputs.shape
    width = features * rows
    span = tokens_col // rows
    head_dim = b_value.shape[0]
    kv_cols = w_keyval.shape[1]
    head_cols = w_query.shape[1]
    query_cols = head_cols * cols // rows
    heads_each = head_cols // query_cols

    up_cols = w_up.shape[1]

    vectors = jnp.stack([first_gain, first_shift, b_out, second_gain, second_shift, b_down])
    vectors = in_parts(padded(vectors, 8), 3).reshape(24, features)
    steps_x = row_gather(jnp.concatenate([inputs, padded(vectors, 32)], 0))
    fly_x = next(steps_x)
    kv_local = w_keyval.reshape(-1, query_cols)
    fly_kv = col_parts(kv_local)
    fly_x, fly_kv = barrier(fly_x, fly_kv)

    fly_x = advance(steps_x, fly_x)
    kv_strip = jnp.transpose(
        col_join(kv_local, fly_kv).reshape(cols, features, kv_cols), (1, 0, 2)
    ).reshape(features, cols * kv_cols)
    steps_kv = row_gather(kv_strip)
    fly_kv = next(steps_kv)
    query_local = jnp.transpose(w_query.reshape(features, heads_each, query_cols), (1, 0, 2))
    fly_q = col_parts(query_local)
    bias_local = b_query.reshape(heads_each, query_cols)
    fly_bias = col_parts(bias_local)
    fly_x, fly_kv = barrier(fly_x, fly_kv)

    w_up_late, _ = barrier(w_up, fly_x)
    w_up_all = lax.all_gather(w_up_late, "row", axis=0, tiled=True)

    fly_x = advance(steps_x, fly_x)
    fly_kv = advance(steps_kv, fly_kv)
    w_out_late, _ = barrier(w_out, fly_bias)
    fly_out = col_parts(w_out_late)
    fly_x, fly_kv = barrier(fly_x, fly_kv)

    fly_kv = advance(steps_kv, fly_kv)
    cot_late, _ = barrier(cotangent, fly_x)
    cot_own = lax.all_to_all(cot_late, "row", 0, 1, tiled=True)
    mine, theirs = finish(steps_x, fly_x)
    first_all, own_low, vectors = norm_gathered(mine, theirs, tokens_col, span)
    gain1, shift1, bias_out, gain2, shift2, bias_down = (vectors[k : k + 1] for k in range(6))
    first_all, own_low, fly_kv, fly_q, fly_bias, cot_own = barrier(
        first_all, own_low, fly_kv, fly_q, fly_bias, cot_own
    )

    w_kv_all = in_row_order(jnp.concatenate(finish(steps_kv, fly_kv), 0), 0)
    own = own_low.astype(F32)
    first_low = lax.dynamic_slice_in_dim(first_all, row * span, span, 0)
    kv_own = dot_plain(first_low, w_kv_all).astype(BF16)
    fly_kv = col_parts(kv_own)
    query_flat = col_join(query_local, fly_q).reshape(rows, features, query_cols)
    w_query_row = exchange_rows(query_flat)
    bias_query = lax.dynamic_slice(
        col_join(bias_local, fly_bias), (row // heads_each, row % heads_each, 0), (1, 1, query_cols)
    ).reshape(1, query_cols)
    fly_kv, w_query_row = barrier(fly_kv, w_query_row)
    steps_kv = row_gather(col_join(kv_own, fly_kv).reshape(cols * span, -1))
    fly_kv = next(steps_kv)
    w_out_all = lax.all_gather(
        col_join(w_out, fly_out).reshape(cols * head_cols, features), "row", axis=1, tiled=True
    )
    queries = (dot_plain(first_all, w_query_row.reshape(width, query_cols)) + bias_query).astype(
        BF16
    )
    fly_kv, queries = barrier(fly_kv, queries)
    fly_cot = col_parts(cot_own)
    kv_all = jnp.concatenate(finish(steps_kv, advance(steps_kv, fly_kv)), 0)
    queries, kv_all, w_up_all = barrier(queries, kv_all, w_up_all)

    attend, attend_back = attention_calls(seq_blocks, tokens_col, span, head_dim, query_cols)
    core_turned, logs, attn_low = attend(queries, kv_all, b_value[None, :])
    attn_own = lax.all_to_all(attn_low, "row", 0, 1, tiled=True)
    attn_own, w_out_all, fly_cot = barrier(attn_own, w_out_all, fly_cot)
    w_down_late, _ = barrier(w_down, w_out_all)
    w_down_all = lax.all_gather(w_down_late, "row", axis=1, tiled=True)
    middle = own + dot_plain(attn_own, w_out_all) + bias_out

    normed2, scale2 = norm_forward(middle)
    second_low = (normed2 * gain2 + shift2).astype(BF16)
    fly_second = col_parts(second_low)
    query_strip = jnp.transpose(query_flat, (1, 0, 2)).reshape(features, rows * query_cols)
    query_strip, _ = barrier(query_strip, w_down_all)
    w_query_all = lax.all_gather(query_strip, "row", axis=0, tiled=True)
    cot_all = col_join(cot_own, fly_cot).reshape(cols * span, width)
    fly_second, cot_all, w_down_all = barrier(fly_second, cot_all, w_down_all)
    second_all = col_join(second_low, fly_second).reshape(cols * span, width)
    grad_hidden = dot_last(cot_all, w_down_all)
    pre = dot_plain(second_all, w_up_all) + b_up
    gelu_value, gelu_back = jax.vjp(partial(jax.nn.gelu, approximate=True), pre)
    hidden = gelu_value.astype(BF16)
    grad_pre = gelu_back(grad_hidden)[0].astype(BF16)
    fly_second = col_send(dot_last(grad_pre, w_up_all).reshape(cols, span, width))
    down_part = dot_first(hidden, cot_all).astype(BF16)
    up_part = dot_first(second_all, grad_pre).astype(BF16)
    grad_w_down = lax.psum_scatter(down_part, "row", scatter_dimension=1, tiled=True).astype(F32)
    grad_w_up = lax.psum_scatter(up_part, "row", scatter_dimension=0, tiled=True).astype(F32)
    fly_second, _, _, w_query_all = barrier(fly_second, down_part, up_part, w_query_all)

    grad_in2, gain2_part, shift2_part = norm_backward(add_up(fly_second), normed2, scale2, gain2)
    grad_middle = cot_own.astype(F32) + grad_in2
    mid_low = grad_middle.astype(BF16)
    grad_attn_own = dot_last(mid_low, w_out_all).astype(BF16)
    grad_attn = lax.all_to_all(grad_attn_own, "row", 1, 0, tiled=True)
    steps_mid = row_gather(mid_low)
    fly_mid = next(steps_mid)
    late_hidden, _ = barrier(hidden, mid_low)
    out_part = dot_plain(late_hidden, w_down_all).astype(BF16)
    grad_attn, fly_mid, out_part = barrier(grad_attn, fly_mid, out_part)
    fly_mid = advance(steps_mid, fly_mid)
    fly_block = col_send(out_part.reshape(cols, span, width))

    grad_queries, key_mine, key_theirs, value_mine, value_theirs = attend_back(
        queries, grad_attn, core_turned, logs, kv_all
    )
    grad_queries, key_theirs, value_theirs, fly_mid = barrier(
        grad_queries, key_theirs, value_theirs, fly_mid
    )

    steps_kv = row_scatter([key_mine, value_mine], [key_theirs, value_theirs])
    fly_kv = next(steps_kv)
    queries_own = lax.all_to_all(grad_queries, "row", 0, 1, tiled=True)
    fly_mid = advance(steps_mid, fly_mid)
    query_part = dot_first(first_all, grad_queries).astype(BF16)
    fly_kv, fly_mid, query_part = barrier(fly_kv, fly_mid, query_part)
    fly_kv = advance(steps_kv, fly_kv)
    mid_mine, mid_theirs = finish(steps_mid, fly_mid)
    attn_tokens = attn_low.reshape(rows, span, query_cols)
    apart = [2 * k for k in range(rows // 2)]

    def attn_rows(offset):
        return jnp.concatenate(
            [
                lax.dynamic_index_in_dim(attn_tokens, row ^ (p + offset), 0, keepdims=False)
                for p in apart
            ],
            0,
        )

    out_part = (
        dot_first(mid_mine.reshape(-1, width), attn_rows(0))
        + dot_first(mid_theirs.reshape(-1, width), attn_rows(1))
    ).astype(BF16)
    query_bias = padded(in_parts(jnp.sum(grad_queries.astype(F32), 0), 2), 16)
    up_bias = in_parts(jnp.sum(grad_pre.astype(F32), 0), 2).reshape(-1, query_cols)
    up_rows = up_bias.shape[0]
    extra = jnp.concatenate([query_bias, padded(up_bias, 16)], 0)
    fly_kv, queries_own, out_part = barrier(fly_kv, queries_own, out_part)
    fly_kv = advance(steps_kv, fly_kv)
    first_part = dot_last(queries_own, w_query_all)
    weights = exchange_rows(
        jnp.concatenate(
            [
                query_part.reshape(rows, features, query_cols),
                out_part.reshape(rows, features, query_cols),
                jnp.broadcast_to(extra[None], (rows,) + extra.shape),
            ],
            1,
        )
    )
    fly_kv, fly_block, first_part = barrier(fly_kv, fly_block, first_part)
    kv_group = jnp.concatenate(finish(steps_kv, fly_kv), -1)
    fly_kv = col_send(kv_group.reshape(cols, span, -1))
    out_own = (middle + add_up(fly_block) + bias_down).astype(BF16)
    fly_kv, weights = barrier(fly_kv, weights)

    both = 2 * features + 16
    fly_weights = col_send(weights[:, :both].reshape(cols, heads_each, both, query_cols))
    up_total = total(weights[:, both : both + up_rows]).reshape(2, up_cols)
    kv_mine = add_up(fly_kv).astype(BF16)
    grad_first = first_part + dot_last(kv_mine, w_kv_all)
    kv_part = dot_first(first_low, kv_mine).astype(BF16)
    normed1, scale1 = norm_forward(own)
    grad_in1, gain1_part, shift1_part = norm_backward(grad_first, normed1, scale1, gain1)
    feature_parts = jnp.stack(
        [
            gain1_part,
            shift1_part,
            gain2_part,
            shift2_part,
            jnp.sum(mid_low.astype(F32), 0),
            jnp.sum(cot_own.astype(F32), 0),
        ]
    )
    value_part = jnp.sum(grad_attn_own.astype(F32).reshape(-1, head_dim), 0)
    value_rows = jnp.broadcast_to(
        jnp.pad(in_parts(value_part, 2), ((0, 0), (0, features - head_dim)))[None],
        (rows, 2, features),
    )
    feature_rows = jnp.transpose(
        in_parts(feature_parts, 2).reshape(12, rows, features), (1, 0, 2)
    )
    grad_low = jnp.transpose(
        (grad_middle + grad_in1).astype(BF16).reshape(span, rows, features), (1, 0, 2)
    )
    kv_wide = kv_part.reshape(rows, -1, features)
    kv_rows = kv_wide.shape[1]
    last = exchange_rows(
        jnp.concatenate(
            [
                grad_low,
                kv_wide,
                feature_rows,
                value_rows,
                jnp.zeros((rows, 2, features), BF16),
            ],
            1,
        )
    )
    block_output = lax.all_to_all(out_own, "row", 1, 0, tiled=True)
    grad_inputs = last[:, :span].reshape(tokens_col, features).astype(F32)
    kv_sum = total(last[:, span : span + kv_rows]).reshape(features, cols, kv_cols)
    grad_w_keyval = add_up(col_send(jnp.transpose(kv_sum, (1, 0, 2))))
    sums = total(last[:, span + kv_rows : span + kv_rows + 16])
    sums = add_up([sums] + col_parts(sums))
    by_feature = sums[0:6] + sums[6:12]
    grad_b_value = (sums[12] + sums[13])[:head_dim]

    weights = add_up(fly_weights)
    grad_w_query = jnp.transpose(weights[:, :features], (1, 0, 2)).reshape(features, head_cols)
    grad_w_out = jnp.transpose(weights[:, features : 2 * features], (0, 2, 1)).reshape(
        head_cols, features
    )
    grad_b_query = (weights[:, 2 * features] + weights[:, 2 * features + 1]).reshape(head_cols)
    return (
        block_output,
        grad_inputs,
        by_feature[0],
        by_feature[1],
        grad_w_query,
        grad_b_query,
        grad_w_keyval,
        grad_b_value,
        grad_w_out,
        by_feature[4],
        by_feature[2],
        by_feature[3],
        grad_w_up,
        up_total[0] + up_total[1],
        grad_w_down,
        by_feature[5],
    )


def solution(mesh):
    both, rows, cols = P("col", "row"), P("row"), P("col")
    return jax.shard_map(
        body,
        mesh=mesh,
        in_specs=(
            both, both, P(), rows, rows, P("row", "col"), cols, P("row", "col"), P(), both, rows,
            rows, rows, P("row", "col"), cols, both, rows,
        ),
        out_specs=(
            both, both, rows, rows, P("row", "col"), cols, P("row", "col"), P(), both, rows,
            rows, rows, P("row", "col"), cols, both, rows,
        ),
        check_vma=False,
    )
```

```python
from functools import partial

import jax
import jax.numpy as jnp
from jax import lax
from jax.experimental import pallas as pl
from jax.experimental.pallas import tpu as pltpu
from jax.sharding import PartitionSpec as P

BLK = 256
EPSILON = 1e-05
NEGATIVE = -1e30
LOG2E = 1.4426950408889634
F32 = jnp.float32
BF16 = jnp.bfloat16


def barrier(*values):
    return lax.optimization_barrier(values)


def col_parts(value):
    count = lax.axis_size("col")
    return [
        lax.ppermute(value, "col", [(i, (i + step) % count) for i in range(count)])
        for step in range(1, count)
    ]


def col_join(value, parts):
    count = lax.axis_size("col")
    me = lax.axis_index("col")
    out = jnp.zeros((count,) + value.shape, value.dtype)
    out = lax.dynamic_update_index_in_dim(out, value, me, 0)
    for step, part in enumerate(parts, 1):
        out = lax.dynamic_update_index_in_dim(out, part, lax.rem(me - step + count, count), 0)
    return out


def col_send(pieces):
    count = lax.axis_size("col")
    me = lax.axis_index("col")
    low = pieces.astype(BF16)
    out = [lax.dynamic_index_in_dim(low, me, 0, keepdims=False)]
    for step in range(1, count):
        part = lax.dynamic_index_in_dim(low, lax.rem(me + step, count), 0, keepdims=False)
        out.append(
            lax.ppermute(part, "col", [(i, (i + step) % count) for i in range(count)])
        )
    return out


def add_up(parts):
    return sum(part.astype(F32) for part in parts)


def exchange_rows(pieces):
    return lax.all_to_all(pieces.astype(BF16), "row", 0, 0)


def total(pieces):
    return jnp.sum(pieces.astype(F32), 0)


def swap(value, bit):
    count = lax.axis_size("row")
    return lax.ppermute(value, "row", [(i, i ^ bit) for i in range(count)])


def chip_bits():
    bits = []
    bit = 2
    while bit < lax.axis_size("row"):
        bits.append(bit)
        bit *= 2
    return bits


def row_place(other):
    apart = jnp.bitwise_xor(lax.axis_index("row"), other)
    return (apart & 1) * (lax.axis_size("row") // 2) + (apart >> 1)


def in_row_order(pieces, axis):
    count = pieces.shape[0]
    return jnp.concatenate(
        [
            lax.dynamic_index_in_dim(pieces, row_place(a), 0, keepdims=False)
            for a in range(count)
        ],
        axis,
    )


def row_gather(value, hold=list):
    half = value.shape[-1] // 2
    bits = chip_bits()
    orders = (bits, bits[::-1])
    held = [{0: value[..., :half]}, {0: value[..., half:]}]
    for step in range(len(bits)):
        keys = [sorted(h) for h in held]
        ready = hold([jnp.stack([h[k] for k in ks]) for h, ks in zip(held, keys)])
        got = yield [swap(part, order[step]) for part, order in zip(ready, orders)]
        for h, ks, order, new in zip(held, keys, orders, got):
            h.update({k ^ order[step]: new[n] for n, k in enumerate(ks)})
    own = jnp.stack([jnp.concatenate([held[0][k], held[1][k]], -1) for k in sorted(held[0])])
    (other,) = yield [swap(own, 1)]
    return own, other


def row_scatter(mine, theirs):
    got = yield [swap(part, 1) for part in theirs]
    bits = chip_bits()
    orders = (bits[::-1], bits)
    held = []
    for part, new in zip(mine, got):
        both = part + new.astype(F32)
        held.append({2 * k: both[k] for k in range(both.shape[0])})
    for step in range(len(bits)):
        keeps = [sorted(k for k in h if not k & order[step]) for h, order in zip(held, orders)]
        got = yield [
            swap(jnp.stack([h[k ^ order[step]] for k in keep]).astype(BF16), order[step])
            for h, keep, order in zip(held, keeps, orders)
        ]
        held = [
            {k: h[k] + new[n].astype(F32) for n, k in enumerate(keep)}
            for h, keep, new in zip(held, keeps, got)
        ]
    return [h[0] for h in held]


def advance(steps, arrived):
    try:
        return steps.send(list(arrived))
    except StopIteration as stop:
        return {"done": stop.value}


def finish(steps, arrived):
    while True:
        arrived = advance(steps, list(barrier(*arrived)))
        if isinstance(arrived, dict):
            return arrived["done"]


def in_parts(vector, count):
    parts = []
    for _ in range(count):
        low = lax.reduce_precision(vector, 8, 7)
        parts.append(low.astype(BF16))
        vector = vector - low
    return jnp.stack(parts)


def padded(rows_array, multiple):
    short = -rows_array.shape[0] % multiple
    return jnp.pad(rows_array, ((0, short), (0, 0)))


def norm_kernel(
    me_ref, mine_ref, theirs_ref, mine_vec, theirs_vec, mine_own, theirs_own,
    first_ref, own_ref, vector_ref,
    *, width
):
    half = mine_ref.shape[0]
    features = mine_ref.shape[2]
    places = [(mine_ref, mine_vec, mine_own, 2 * k, k) for k in range(half)]
    places += [(theirs_ref, theirs_vec, theirs_own, 2 * k + 1, k) for k in range(half)]
    me = me_ref[0]

    def columns(apart):
        return pl.ds(pl.multiple_of(jnp.bitwise_xor(me, apart) * features, features), features)

    @pl.when(pl.program_id(0) == 0)
    def _():
        for _, vec, own, apart, k in places:
            stack = vec[k].astype(F32)
            vector_ref[:, columns(apart)] = stack[0:8] + stack[8:16] + stack[16:24]
            own_ref[:, columns(apart)] = own[k]

    sums = sum(jnp.sum(ref[k].astype(F32), 1, keepdims=True) for ref, _, _, _, k in places)
    mean = sums / width
    squares = jnp.zeros_like(mean)
    for ref, _, _, _, k in places:
        centred = ref[k].astype(F32) - mean
        squares = squares + jnp.sum(centred * centred, 1, keepdims=True)
    scale = lax.rsqrt(squares / width + EPSILON)
    for ref, vec, _, apart, k in places:
        stack = vec[k].astype(F32)
        both = stack[0:8] + stack[8:16] + stack[16:24]
        normed = (ref[k].astype(F32) - mean) * scale
        first_ref[:, columns(apart)] = (normed * both[0:1] + both[1:2]).astype(BF16)


def norm_gathered(mine, theirs, tokens, span):
    rows = lax.axis_size("row")
    half, _, features = mine.shape
    width = features * rows
    me = jnp.full((1,), lax.axis_index("row"), jnp.int32)
    block = pl.BlockSpec((half, BLK, features), lambda i, _: (0, i, 0))
    vec = pl.BlockSpec((half, 32, features), lambda i, _: (0, tokens // 32, 0))
    own = pl.BlockSpec((half, span, features), lambda i, m: (0, m[0], 0))
    return pl.pallas_call(
        partial(norm_kernel, width=width),
        out_shape=(
            jax.ShapeDtypeStruct((tokens, width), BF16),
            jax.ShapeDtypeStruct((span, width), BF16),
            jax.ShapeDtypeStruct((8, width), F32),
        ),
        grid_spec=pltpu.PrefetchScalarGridSpec(
            num_scalar_prefetch=1,
            grid=(tokens // BLK,),
            in_specs=[block, block, vec, vec, own, own],
            out_specs=(
                pl.BlockSpec((BLK, width), lambda i, _: (i, 0)),
                pl.BlockSpec((span, width), lambda i, _: (0, 0)),
                pl.BlockSpec((8, width), lambda i, _: (0, 0)),
            ),
        ),
        name="norm_gathered",
    )(me, mine, theirs, mine, theirs, mine, theirs)


def stacked_heads(block, head_dim):
    count = block.shape[1] // head_dim
    return jnp.concatenate([block[:, h * head_dim : (h + 1) * head_dim] for h in range(count)], 0)


def dot_last(left, right):
    return lax.dot_general(left, right, (((1,), (1,)), ((), ())), preferred_element_type=F32)


def dot_first(left, right):
    return lax.dot_general(left, right, (((0,), (0,)), ((), ())), preferred_element_type=F32)


def dot_plain(left, right):
    return lax.dot_general(left, right, (((1,), (0,)), ((), ())), preferred_element_type=F32)


def key_pieces(kb, me, per_col, per_block, half):
    col = lax.div(kb, per_col)
    first = lax.rem(kb, per_col) * per_block
    places = []
    for t in range(per_block):
        apart = jnp.bitwise_xor(first + t, me)
        places.append((apart & 1) * half + lax.shift_right_logical(apart, 1))
    return col, places


def forward_kernel(
    low_ref, high_ref, me_ref, q_ref, kv_ref, bias_ref, out_ref, log_ref, low_out_ref, acc_ref, top_ref, sum_ref,
    *, head_dim, per_col, per_block, span
):
    chunk = pl.program_id(0)
    q = stacked_heads(q_ref[...], head_dim)
    rows = q.shape[0]
    acc_ref[...] = jnp.zeros_like(acc_ref)
    top_ref[...] = jnp.full_like(top_ref, NEGATIVE)
    sum_ref[...] = jnp.zeros_like(sum_ref)
    factor = head_dim ** (-0.5) * LOG2E

    def visit(kb, carry):
        col, places = key_pieces(kb, me_ref[0], per_col, per_block, kv_ref.shape[0] // 2)
        at = pl.ds(pl.multiple_of(col * span, span), span)
        kv = jnp.concatenate([kv_ref[place, at, :] for place in places], 0)
        scores = dot_last(kv[:, :head_dim], q) * factor
        old = top_ref[...]
        new = jnp.maximum(old, jnp.max(scores, 0, keepdims=True))
        weights = jnp.exp2(scores - new)
        decay = jnp.exp2(old - new)
        top_ref[...] = new
        sum_ref[...] = sum_ref[...] * decay + jnp.sum(weights, 0, keepdims=True)
        acc_ref[...] = acc_ref[...] * decay + dot_first(kv[:, head_dim:], weights.astype(BF16))
        return carry

    lax.fori_loop(low_ref[chunk], high_ref[chunk], visit, 0)
    out = acc_ref[...] / sum_ref[...]
    out_ref[0] = out
    for h in range(rows // BLK):
        low_out_ref[:, h * head_dim : (h + 1) * head_dim] = (
            jnp.transpose(out[:, h * BLK : (h + 1) * BLK]) + bias_ref[...]
        ).astype(BF16)
    log_ref[0] = top_ref[...] + jnp.log2(sum_ref[...])


def backward_kernel(
    low_ref, high_ref, me_ref, q_ref, grad_ref, out_ref, log_ref, kv_ref, gq_ref, gk_mine, gk_theirs, gv_mine, gv_theirs,
    gk_acc, gv_acc, gq_acc,
    *, head_dim, per_col, per_block, span
):
    chunk = pl.program_id(0)

    @pl.when(chunk == 0)
    def _():
        gk_acc[...] = jnp.zeros_like(gk_acc)
        gv_acc[...] = jnp.zeros_like(gv_acc)

    q = stacked_heads(q_ref[...], head_dim)
    grad = stacked_heads(grad_ref[...], head_dim)
    scale = head_dim ** (-0.5)
    log = log_ref[0]
    delta = jnp.sum(out_ref[0] * jnp.transpose(grad.astype(F32)), 0, keepdims=True)
    gq_acc[...] = jnp.zeros_like(gq_acc)

    def visit(kb, carry):
        col, places = key_pieces(kb, me_ref[0], per_col, per_block, kv_ref.shape[0] // 2)
        at = pl.ds(pl.multiple_of(col * span, span), span)
        kv = jnp.concatenate([kv_ref[place, at, :] for place in places], 0)
        keys, vals = kv[:, :head_dim], kv[:, head_dim:]
        scores = dot_last(keys, q) * (scale * LOG2E)
        probs = jnp.exp2(scores - log)
        grad_probs = dot_last(vals, grad)
        grad_scores = (probs * (grad_probs - delta)).astype(BF16)
        gq_acc[...] += dot_first(keys, grad_scores)
        gk = dot_plain(grad_scores, q)
        gv = dot_plain(probs.astype(BF16), grad)
        for t, place in enumerate(places):
            gk_acc[place, at, :] += gk[t * span : (t + 1) * span]
            gv_acc[place, at, :] += gv[t * span : (t + 1) * span]
        return carry

    lax.fori_loop(low_ref[chunk], high_ref[chunk], visit, 0)
    gq = gq_acc[...] * scale
    for h in range(q.shape[0] // BLK):
        gq_ref[:, h * head_dim : (h + 1) * head_dim] = jnp.transpose(
            gq[:, h * BLK : (h + 1) * BLK]
        ).astype(BF16)

    @pl.when(chunk == pl.num_programs(0) - 1)
    def _():
        half = gk_mine.shape[0]
        gk_mine[...] = gk_acc[:half] * scale
        gk_theirs[...] = (gk_acc[half:] * scale).astype(BF16)
        gv_mine[...] = gv_acc[:half]
        gv_theirs[...] = gv_acc[half:].astype(BF16)


def attention_calls(seq_blocks, tokens_col, span, head_dim, query_cols):
    rows, cols = lax.axis_size("row"), lax.axis_size("col")
    per_col, per_block = tokens_col // BLK, BLK // span
    heads = query_cols // head_dim
    me = lax.axis_index("row")
    ends = jnp.cumsum(seq_blocks)
    blocks = lax.axis_index("col") * per_col + jnp.arange(per_col, dtype=jnp.int32)
    owner = jnp.sum((blocks[:, None] >= ends[None, :]).astype(jnp.int32), 1)
    starts = ends - seq_blocks
    low = jnp.sum(
        jnp.where(owner[:, None] == jnp.arange(ends.shape[0])[None, :], starts[None, :], 0), 1
    ).astype(jnp.int32)
    scalars = (low, (blocks + 1).astype(jnp.int32), jnp.full((1,), me, jnp.int32))
    sizes = dict(head_dim=head_dim, per_col=per_col, per_block=per_block, span=span)
    chunk_rows = pl.BlockSpec((BLK, query_cols), lambda c, *_: (c, 0))
    whole_kv = pl.BlockSpec((rows, cols * span, 2 * head_dim), lambda c, *_: (0, 0, 0))
    half_kv = pl.BlockSpec((rows // 2, cols * span, head_dim), lambda c, *_: (0, 0, 0))
    turned = pl.BlockSpec((1, head_dim, heads * BLK), lambda c, *_: (c, 0, 0))
    logs = pl.BlockSpec((1, 1, heads * BLK), lambda c, *_: (c, 0, 0))
    bias = pl.BlockSpec((1, head_dim), lambda c, *_: (0, 0))
    shape = jax.ShapeDtypeStruct

    def forward(queries, key_values, bias_value):
        return pl.pallas_call(
            partial(forward_kernel, **sizes),
            out_shape=(
                shape((per_col, head_dim, heads * BLK), F32),
                shape((per_col, 1, heads * BLK), F32),
                shape((tokens_col, query_cols), BF16),
            ),
            grid_spec=pltpu.PrefetchScalarGridSpec(
                num_scalar_prefetch=3,
                grid=(per_col,),
                in_specs=[chunk_rows, whole_kv, bias],
                out_specs=(turned, logs, chunk_rows),
                scratch_shapes=[
                    pltpu.VMEM((head_dim, heads * BLK), F32),
                    pltpu.VMEM((1, heads * BLK), F32),
                    pltpu.VMEM((1, heads * BLK), F32),
                ],
            ),
            name="attend_forward",
        )(*scalars, queries, key_values, bias_value)

    def backward(queries, grad_low, out, log, key_values):
        return pl.pallas_call(
            partial(backward_kernel, **sizes),
            out_shape=(
                shape((tokens_col, query_cols), BF16),
                shape((rows // 2, cols * span, head_dim), F32),
                shape((rows // 2, cols * span, head_dim), BF16),
                shape((rows // 2, cols * span, head_dim), F32),
                shape((rows // 2, cols * span, head_dim), BF16),
            ),
            grid_spec=pltpu.PrefetchScalarGridSpec(
                num_scalar_prefetch=3,
                grid=(per_col,),
                in_specs=[chunk_rows, chunk_rows, turned, logs, whole_kv],
                out_specs=(chunk_rows, half_kv, half_kv, half_kv, half_kv),
                scratch_shapes=[
                    pltpu.VMEM((rows, cols * span, head_dim), F32),
                    pltpu.VMEM((rows, cols * span, head_dim), F32),
                    pltpu.VMEM((head_dim, heads * BLK), F32),
                ],
            ),
            name="attend_backward",
        )(*scalars, queries, grad_low, out, log, key_values)

    return forward, backward


def norm_forward(values):
    mean = jnp.mean(values, 1, keepdims=True)
    centred = values - mean
    scale = lax.rsqrt(jnp.mean(centred * centred, 1, keepdims=True) + EPSILON)
    return centred * scale, scale


def norm_backward(grad_out, normed, scale, gain):
    grad_normed = grad_out * gain
    plain = jnp.mean(grad_normed, 1, keepdims=True)
    cross = jnp.mean(grad_normed * normed, 1, keepdims=True)
    grad_in = scale * (grad_normed - plain - normed * cross)
    return grad_in, jnp.sum(grad_out * normed, 0), jnp.sum(grad_out, 0)


def body(
    inputs,
    cotangent,
    seq_blocks,
    first_gain,
    first_shift,
    w_query,
    b_query,
    w_keyval,
    b_value,
    w_out,
    b_out,
    second_gain,
    second_shift,
    w_up,
    b_up,
    w_down,
    b_down,
):
    rows, cols = lax.axis_size("row"), lax.axis_size("col")
    row, col = lax.axis_index("row"), lax.axis_index("col")
    tokens_col, features = inputs.shape
    width = features * rows
    span = tokens_col // rows
    head_dim = b_value.shape[0]
    kv_cols = w_keyval.shape[1]
    head_cols = w_query.shape[1]
    query_cols = head_cols * cols // rows
    heads_each = head_cols // query_cols

    up_cols = w_up.shape[1]

    vectors = jnp.stack([first_gain, first_shift, b_out, second_gain, second_shift, b_down])
    vectors = in_parts(padded(vectors, 8), 3).reshape(24, features)
    steps_x = row_gather(jnp.concatenate([inputs, padded(vectors, 32)], 0))
    fly_x = next(steps_x)
    kv_local = w_keyval.reshape(-1, query_cols)
    local_rows = kv_local.shape[0]
    bias_local = in_parts(b_query.reshape(heads_each, query_cols), 3).reshape(-1, query_cols)
    bias_rows = bias_local.shape[0]
    kv_local = jnp.concatenate([kv_local, padded(bias_local, 16)], 0)
    fly_kv = col_parts(kv_local)
    query_local = jnp.transpose(w_query.reshape(features, heads_each, query_cols), (1, 0, 2))
    fly_x, fly_kv, query_local, w_up_late, w_out_late = barrier(
        fly_x, fly_kv, query_local, w_up, w_out
    )

    w_up_all = lax.all_gather(w_up_late, "row", axis=0, tiled=True)
    fly_q = col_parts(query_local)
    fly_out = col_parts(w_out_late)
    fly_x = advance(steps_x, fly_x)
    kv_join = col_join(kv_local, fly_kv)
    kv_strip = jnp.transpose(
        kv_join[:, :local_rows].reshape(cols, features, kv_cols), (1, 0, 2)
    ).reshape(features, cols * kv_cols)
    bias_parts = lax.dynamic_index_in_dim(
        kv_join[:, local_rows : local_rows + bias_rows], row // heads_each, 0, keepdims=False
    ).reshape(3, heads_each, query_cols)
    bias_query = jnp.sum(
        lax.dynamic_index_in_dim(bias_parts, row % heads_each, 1, keepdims=True).astype(F32), 0
    )
    steps_kv = row_gather(kv_strip)
    fly_kv = next(steps_kv)
    fly_x, fly_kv, fly_q = barrier(fly_x, fly_kv, fly_q)

    query_flat = col_join(query_local, fly_q).reshape(rows, features, query_cols)
    w_query_row = exchange_rows(query_flat)
    fly_x = advance(steps_x, fly_x)
    fly_kv = advance(steps_kv, fly_kv)
    fly_x, fly_kv = barrier(fly_x, fly_kv)

    fly_kv = advance(steps_kv, fly_kv)
    mine, theirs = finish(steps_x, fly_x)
    first_all, own_low, vectors = norm_gathered(mine, theirs, tokens_col, span)
    gain1, shift1, bias_out, gain2, shift2, bias_down = (vectors[k : k + 1] for k in range(6))
    first_all, own_low, fly_kv, w_query_row, fly_out, cot_late = barrier(
        first_all, own_low, fly_kv, w_query_row, fly_out, cotangent
    )
    w_out_all = lax.all_gather(
        col_join(w_out, fly_out).reshape(cols * head_cols, features), "row", axis=1, tiled=True
    )

    w_kv_all = in_row_order(jnp.concatenate(finish(steps_kv, fly_kv), 0), 0)
    own = own_low.astype(F32)
    first_low = lax.dynamic_slice_in_dim(first_all, row * span, span, 0)
    kv_own = dot_plain(first_low, w_kv_all).astype(BF16)
    fly_kv = col_parts(kv_own)
    cot_own = lax.all_to_all(cot_late, "row", 0, 1, tiled=True)
    (fly_kv,) = barrier(fly_kv)
    steps_kv = row_gather(col_join(kv_own, fly_kv).reshape(cols * span, -1))
    fly_kv = next(steps_kv)
    queries = (dot_plain(first_all, w_query_row.reshape(width, query_cols)) + bias_query).astype(
        BF16
    )
    kv_all = jnp.concatenate(finish(steps_kv, fly_kv), 0)
    queries, kv_all, cot_own, w_up_all = barrier(queries, kv_all, cot_own, w_up_all)
    fly_cot = col_parts(cot_own)
    w_down_late, _ = barrier(w_down, queries)
    w_down_all = lax.all_gather(w_down_late, "row", axis=1, tiled=True)

    attend, attend_back = attention_calls(seq_blocks, tokens_col, span, head_dim, query_cols)
    core_turned, logs, attn_low = attend(queries, kv_all, b_value[None, :])
    attn_own = lax.all_to_all(attn_low, "row", 0, 1, tiled=True)
    attn_own, w_out_all, fly_cot = barrier(attn_own, w_out_all, fly_cot)
    middle = own + dot_plain(attn_own, w_out_all) + bias_out

    normed2, scale2 = norm_forward(middle)
    second_low = (normed2 * gain2 + shift2).astype(BF16)
    fly_second = col_parts(second_low)
    query_strip = jnp.transpose(query_flat, (1, 0, 2)).reshape(features, rows * query_cols)
    query_strip, _ = barrier(query_strip, second_low)
    w_query_all = lax.all_gather(query_strip, "row", axis=0, tiled=True)
    cot_all = col_join(cot_own, fly_cot).reshape(cols * span, width)
    fly_second, cot_all = barrier(fly_second, cot_all)
    second_all = col_join(second_low, fly_second).reshape(cols * span, width)
    pre = dot_plain(second_all, w_up_all) + b_up
    grad_hidden = dot_last(cot_all, w_down_all)
    gelu_value, gelu_back = jax.vjp(partial(jax.nn.gelu, approximate=True), pre)
    hidden = gelu_value.astype(BF16)
    grad_pre = gelu_back(grad_hidden)[0].astype(BF16)
    second_part = dot_last(grad_pre, w_up_all).reshape(cols, span, width).astype(BF16)
    second_part, hidden, grad_pre = barrier(second_part, hidden, grad_pre)
    fly_second = col_send(second_part)
    hidden_late, _ = barrier(hidden, fly_second[1])
    up_part = dot_first(second_all, grad_pre).astype(BF16)
    down_part = dot_first(hidden, cot_all).astype(BF16)
    grad_w_down = lax.psum_scatter(down_part, "row", scatter_dimension=1, tiled=True).astype(F32)
    grad_w_up = lax.psum_scatter(up_part, "row", scatter_dimension=0, tiled=True).astype(F32)
    out_part = dot_plain(hidden_late, w_down_all).astype(BF16)
    fly_second, _, _, out_part = barrier(fly_second, down_part, up_part, out_part)
    fly_block = col_send(out_part.reshape(cols, span, width))

    grad_in2, gain2_part, shift2_part = norm_backward(add_up(fly_second), normed2, scale2, gain2)
    grad_middle = cot_own.astype(F32) + grad_in2
    mid_low = grad_middle.astype(BF16)
    late = {}

    def hold(ready):
        if "grad_attn" in late:
            ready, late["grad_attn"] = barrier(ready, late["grad_attn"])
        return list(ready)

    steps_mid = row_gather(mid_low, hold)
    fly_mid = next(steps_mid)
    grad_attn_own = dot_last(mid_low, w_out_all).astype(BF16)
    fly_mid, grad_attn_own = barrier(fly_mid, grad_attn_own)
    late["grad_attn"] = lax.all_to_all(grad_attn_own, "row", 1, 0, tiled=True)
    fly_mid = advance(steps_mid, fly_mid)
    grad_attn = late.pop("grad_attn")

    grad_queries, key_mine, key_theirs, value_mine, value_theirs = attend_back(
        queries, grad_attn, core_turned, logs, kv_all
    )
    grad_queries, key_theirs, value_theirs, fly_mid, fly_block = barrier(
        grad_queries, key_theirs, value_theirs, fly_mid, fly_block
    )

    queries_own = lax.all_to_all(grad_queries, "row", 0, 1, tiled=True)
    steps_kv = row_scatter([key_mine, value_mine], [key_theirs, value_theirs])
    fly_kv = next(steps_kv)
    fly_mid = advance(steps_mid, fly_mid)
    query_part = dot_first(first_all, grad_queries).astype(BF16)
    query_bias = padded(in_parts(jnp.sum(grad_queries.astype(F32), 0), 2), 16)
    up_bias = in_parts(jnp.sum(grad_pre.astype(F32), 0), 2).reshape(-1, query_cols)
    up_rows = up_bias.shape[0]
    extra = jnp.concatenate([query_bias, padded(up_bias, 16)], 0)
    out_own = (middle + add_up(fly_block) + bias_down).astype(BF16)
    attn_tokens = attn_low.reshape(rows, span, query_cols)
    apart = [2 * k for k in range(rows // 2)]

    def attn_rows(offset):
        return jnp.concatenate(
            [
                lax.dynamic_index_in_dim(attn_tokens, row ^ (p + offset), 0, keepdims=False)
                for p in apart
            ],
            0,
        )

    attn_mine, attn_theirs = attn_rows(0), attn_rows(1)
    fly_kv, fly_mid, queries_own, attn_mine, attn_theirs = barrier(
        fly_kv, fly_mid, queries_own, attn_mine, attn_theirs
    )
    fly_kv = advance(steps_kv, fly_kv)
    mid_mine, mid_theirs = finish(steps_mid, fly_mid)
    out_weights = (
        dot_first(mid_mine.reshape(-1, width), attn_mine)
        + dot_first(mid_theirs.reshape(-1, width), attn_theirs)
    ).astype(BF16)
    pieces = jnp.concatenate(
        [
            jnp.transpose(out_own.reshape(span, rows, features), (1, 0, 2)),
            out_weights.reshape(rows, features, query_cols),
            query_part.reshape(rows, features, query_cols),
            jnp.broadcast_to(extra[None], (rows,) + extra.shape),
        ],
        1,
    )
    kv_group = jnp.concatenate(finish(steps_kv, fly_kv), -1)

    pieces, kv_group = barrier(pieces, kv_group)
    fly_kv = col_send(kv_group.reshape(cols, span, -1))
    sent = exchange_rows(pieces)
    kv_mine = add_up(fly_kv).astype(BF16)
    grad_first = dot_last(queries_own, w_query_all) + dot_last(kv_mine, w_kv_all)
    normed1, scale1 = norm_forward(own)
    grad_in1, gain1_part, shift1_part = norm_backward(grad_first, normed1, scale1, gain1)
    feature_parts = jnp.stack(
        [
            gain1_part,
            shift1_part,
            gain2_part,
            shift2_part,
            jnp.sum(mid_low.astype(F32), 0),
            jnp.sum(cot_own.astype(F32), 0),
        ]
    )
    value_part = jnp.sum(grad_attn_own.astype(F32).reshape(-1, head_dim), 0)
    value_rows = jnp.tile(
        jnp.pad(in_parts(value_part, 2), ((0, 0), (0, features - head_dim))), (1, rows)
    )
    stacked = jnp.concatenate(
        [
            (grad_middle + grad_in1).astype(BF16),
            padded(jnp.concatenate([in_parts(feature_parts, 2).reshape(12, width), value_rows], 0), 16),
        ],
        0,
    )
    stacked, kv_mine, sent = barrier(stacked, kv_mine, sent)
    block_output = sent[:, :span].reshape(tokens_col, features)
    last_row = span + 2 * features + 16
    fly_weights = col_send(
        sent[:, span:last_row].reshape(cols, heads_each, 2 * features + 16, query_cols)
    )
    up_total = total(sent[:, last_row : last_row + up_rows]).reshape(2, up_cols)
    last = lax.all_to_all(stacked, "row", 1, 0, tiled=True).reshape(rows, -1, features)
    steps_kv = row_gather(kv_mine)
    kv_tokens = in_row_order(jnp.concatenate(finish(steps_kv, next(steps_kv)), 0), 0)
    first_mine = lax.dynamic_slice_in_dim(first_all, row * features, features, 1)
    kv_sum = dot_first(kv_tokens, first_mine).reshape(cols, kv_cols, features)
    last, kv_sum, grad_w_down, grad_w_up = barrier(last, kv_sum, grad_w_down, grad_w_up)
    grad_inputs = last[:, :span].reshape(tokens_col, features).astype(F32)
    sums = in_parts(total(last[:, -16:]), 2).reshape(32, features)
    fly_sums = col_send(
        jnp.concatenate(
            [kv_sum.astype(BF16), jnp.broadcast_to(sums[None], (cols, 32, features))], 1
        )
    )
    fly_weights, fly_sums = barrier(fly_weights, fly_sums)
    sums = add_up(fly_sums)
    grad_w_keyval = jnp.transpose(sums[:kv_cols])
    sums = sums[kv_cols : kv_cols + 16] + sums[kv_cols + 16 :]
    by_feature = sums[0:6] + sums[6:12]
    grad_b_value = (sums[12] + sums[13])[:head_dim]

    weights = add_up(fly_weights)
    grad_w_out = jnp.transpose(weights[:, :features], (0, 2, 1)).reshape(head_cols, features)
    grad_w_query = jnp.transpose(weights[:, features : 2 * features], (1, 0, 2)).reshape(
        features, head_cols
    )
    grad_b_query = (weights[:, 2 * features] + weights[:, 2 * features + 1]).reshape(head_cols)
    return (
        block_output,
        grad_inputs,
        by_feature[0],
        by_feature[1],
        grad_w_query,
        grad_b_query,
        grad_w_keyval,
        grad_b_value,
        grad_w_out,
        by_feature[4],
        by_feature[2],
        by_feature[3],
        grad_w_up,
        up_total[0] + up_total[1],
        grad_w_down,
        by_feature[5],
    )


def solution(mesh):
    both, rows, cols = P("col", "row"), P("row"), P("col")
    return jax.shard_map(
        body,
        mesh=mesh,
        in_specs=(
            both, both, P(), rows, rows, P("row", "col"), cols, P("row", "col"), P(), both, rows,
            rows, rows, P("row", "col"), cols, both, rows,
        ),
        out_specs=(
            both, both, rows, rows, P("row", "col"), cols, P("row", "col"), P(), both, rows,
            rows, rows, P("row", "col"), cols, both, rows,
        ),
        check_vma=False,
    )
```

```python
from functools import partial

import jax
import jax.numpy as jnp
from jax import lax
from jax.experimental import pallas as pl
from jax.experimental.pallas import tpu as pltpu
from jax.sharding import PartitionSpec as P

BLK = 256
EPSILON = 1e-05
NEGATIVE = -1e30
LOG2E = 1.4426950408889634
F32 = jnp.float32
BF16 = jnp.bfloat16


def barrier(*values):
    return lax.optimization_barrier(values)


def col_parts(value):
    count = lax.axis_size("col")
    return [
        lax.ppermute(value, "col", [(i, (i + step) % count) for i in range(count)])
        for step in range(1, count)
    ]


def col_join(value, parts):
    count = lax.axis_size("col")
    me = lax.axis_index("col")
    out = jnp.zeros((count,) + value.shape, value.dtype)
    out = lax.dynamic_update_index_in_dim(out, value, me, 0)
    for step, part in enumerate(parts, 1):
        out = lax.dynamic_update_index_in_dim(out, part, lax.rem(me - step + count, count), 0)
    return out


def col_send(pieces):
    count = lax.axis_size("col")
    me = lax.axis_index("col")
    low = pieces.astype(BF16)
    out = [lax.dynamic_index_in_dim(low, me, 0, keepdims=False)]
    for step in range(1, count):
        part = lax.dynamic_index_in_dim(low, lax.rem(me + step, count), 0, keepdims=False)
        out.append(
            lax.ppermute(part, "col", [(i, (i + step) % count) for i in range(count)])
        )
    return out


def add_up(parts):
    return sum(part.astype(F32) for part in parts)


def exchange_rows(pieces):
    return lax.all_to_all(pieces.astype(BF16), "row", 0, 0)


def total(pieces):
    return jnp.sum(pieces.astype(F32), 0)


def swap(value, bit):
    count = lax.axis_size("row")
    return lax.ppermute(value, "row", [(i, i ^ bit) for i in range(count)])


def chip_bits():
    bits = []
    bit = 2
    while bit < lax.axis_size("row"):
        bits.append(bit)
        bit *= 2
    return bits


def row_place(other):
    apart = jnp.bitwise_xor(lax.axis_index("row"), other)
    return (apart & 1) * (lax.axis_size("row") // 2) + (apart >> 1)


def in_row_order(pieces, axis):
    count = pieces.shape[0]
    return jnp.concatenate(
        [
            lax.dynamic_index_in_dim(pieces, row_place(a), 0, keepdims=False)
            for a in range(count)
        ],
        axis,
    )


def row_gather(value, hold=list):
    half = value.shape[-1] // 2
    bits = chip_bits()
    orders = (bits, bits[::-1])
    held = [{0: value[..., :half]}, {0: value[..., half:]}]
    for step in range(len(bits)):
        keys = [sorted(h) for h in held]
        ready = hold([jnp.stack([h[k] for k in ks]) for h, ks in zip(held, keys)])
        got = yield [swap(part, order[step]) for part, order in zip(ready, orders)]
        for h, ks, order, new in zip(held, keys, orders, got):
            h.update({k ^ order[step]: new[n] for n, k in enumerate(ks)})
    own = jnp.stack([jnp.concatenate([held[0][k], held[1][k]], -1) for k in sorted(held[0])])
    (other,) = yield [swap(own, 1)]
    return own, other


def row_scatter(mine, theirs):
    got = yield [swap(part, 1) for part in theirs]
    bits = chip_bits()
    orders = (bits[::-1], bits)
    held = []
    for part, new in zip(mine, got):
        both = part + new.astype(F32)
        held.append({2 * k: both[k] for k in range(both.shape[0])})
    for step in range(len(bits)):
        keeps = [sorted(k for k in h if not k & order[step]) for h, order in zip(held, orders)]
        got = yield [
            swap(jnp.stack([h[k ^ order[step]] for k in keep]).astype(BF16), order[step])
            for h, keep, order in zip(held, keeps, orders)
        ]
        held = [
            {k: h[k] + new[n].astype(F32) for n, k in enumerate(keep)}
            for h, keep, new in zip(held, keeps, got)
        ]
    return [h[0] for h in held]


def advance(steps, arrived):
    try:
        return steps.send(list(arrived))
    except StopIteration as stop:
        return {"done": stop.value}


def finish(steps, arrived):
    while True:
        arrived = advance(steps, list(barrier(*arrived)))
        if isinstance(arrived, dict):
            return arrived["done"]


def in_parts(vector, count):
    parts = []
    for _ in range(count):
        low = lax.reduce_precision(vector, 8, 7)
        parts.append(low.astype(BF16))
        vector = vector - low
    return jnp.stack(parts)


def padded(rows_array, multiple):
    short = -rows_array.shape[0] % multiple
    return jnp.pad(rows_array, ((0, short), (0, 0)))


def norm_kernel(
    me_ref, mine_ref, theirs_ref, mine_vec, theirs_vec, mine_own, theirs_own,
    first_ref, own_ref, vector_ref,
    *, width
):
    half = mine_ref.shape[0]
    features = mine_ref.shape[2]
    places = [(mine_ref, mine_vec, mine_own, 2 * k, k) for k in range(half)]
    places += [(theirs_ref, theirs_vec, theirs_own, 2 * k + 1, k) for k in range(half)]
    me = me_ref[0]

    def columns(apart):
        return pl.ds(pl.multiple_of(jnp.bitwise_xor(me, apart) * features, features), features)

    @pl.when(pl.program_id(0) == 0)
    def _():
        for _, vec, own, apart, k in places:
            stack = vec[k].astype(F32)
            vector_ref[:, columns(apart)] = stack[0:8] + stack[8:16] + stack[16:24]
            own_ref[:, columns(apart)] = own[k]

    sums = sum(jnp.sum(ref[k].astype(F32), 1, keepdims=True) for ref, _, _, _, k in places)
    mean = sums / width
    squares = jnp.zeros_like(mean)
    for ref, _, _, _, k in places:
        centred = ref[k].astype(F32) - mean
        squares = squares + jnp.sum(centred * centred, 1, keepdims=True)
    scale = lax.rsqrt(squares / width + EPSILON)
    for ref, vec, _, apart, k in places:
        stack = vec[k].astype(F32)
        both = stack[0:8] + stack[8:16] + stack[16:24]
        normed = (ref[k].astype(F32) - mean) * scale
        first_ref[:, columns(apart)] = (normed * both[0:1] + both[1:2]).astype(BF16)


def norm_gathered(mine, theirs, tokens, span):
    rows = lax.axis_size("row")
    half, _, features = mine.shape
    width = features * rows
    me = jnp.full((1,), lax.axis_index("row"), jnp.int32)
    block = pl.BlockSpec((half, BLK, features), lambda i, _: (0, i, 0))
    vec = pl.BlockSpec((half, 32, features), lambda i, _: (0, tokens // 32, 0))
    own = pl.BlockSpec((half, span, features), lambda i, m: (0, m[0], 0))
    return pl.pallas_call(
        partial(norm_kernel, width=width),
        out_shape=(
            jax.ShapeDtypeStruct((tokens, width), BF16),
            jax.ShapeDtypeStruct((span, width), BF16),
            jax.ShapeDtypeStruct((8, width), F32),
        ),
        grid_spec=pltpu.PrefetchScalarGridSpec(
            num_scalar_prefetch=1,
            grid=(tokens // BLK,),
            in_specs=[block, block, vec, vec, own, own],
            out_specs=(
                pl.BlockSpec((BLK, width), lambda i, _: (i, 0)),
                pl.BlockSpec((span, width), lambda i, _: (0, 0)),
                pl.BlockSpec((8, width), lambda i, _: (0, 0)),
            ),
        ),
        name="norm_gathered",
    )(me, mine, theirs, mine, theirs, mine, theirs)


def stacked_heads(block, head_dim):
    count = block.shape[1] // head_dim
    return jnp.concatenate([block[:, h * head_dim : (h + 1) * head_dim] for h in range(count)], 0)


def dot_last(left, right):
    return lax.dot_general(left, right, (((1,), (1,)), ((), ())), preferred_element_type=F32)


def dot_first(left, right):
    return lax.dot_general(left, right, (((0,), (0,)), ((), ())), preferred_element_type=F32)


def dot_plain(left, right):
    return lax.dot_general(left, right, (((1,), (0,)), ((), ())), preferred_element_type=F32)


def key_pieces(kb, me, per_col, per_block, half):
    col = lax.div(kb, per_col)
    first = lax.rem(kb, per_col) * per_block
    places = []
    for t in range(per_block):
        apart = jnp.bitwise_xor(first + t, me)
        places.append((apart & 1) * half + lax.shift_right_logical(apart, 1))
    return col, places


def forward_kernel(
    low_ref, high_ref, me_ref, q_ref, kv_ref, bias_ref, out_ref, log_ref, low_out_ref, acc_ref, top_ref, sum_ref,
    *, head_dim, per_col, per_block, span
):
    chunk = pl.program_id(0)
    q = stacked_heads(q_ref[...], head_dim)
    rows = q.shape[0]
    acc_ref[...] = jnp.zeros_like(acc_ref)
    top_ref[...] = jnp.full_like(top_ref, NEGATIVE)
    sum_ref[...] = jnp.zeros_like(sum_ref)
    factor = head_dim ** (-0.5) * LOG2E

    def visit(kb, carry):
        col, places = key_pieces(kb, me_ref[0], per_col, per_block, kv_ref.shape[0] // 2)
        at = pl.ds(pl.multiple_of(col * span, span), span)
        kv = jnp.concatenate([kv_ref[place, at, :] for place in places], 0)
        scores = dot_last(kv[:, :head_dim], q) * factor
        old = top_ref[...]
        new = jnp.maximum(old, jnp.max(scores, 0, keepdims=True))
        weights = jnp.exp2(scores - new)
        decay = jnp.exp2(old - new)
        top_ref[...] = new
        sum_ref[...] = sum_ref[...] * decay + jnp.sum(weights, 0, keepdims=True)
        acc_ref[...] = acc_ref[...] * decay + dot_first(kv[:, head_dim:], weights.astype(BF16))
        return carry

    lax.fori_loop(low_ref[chunk], high_ref[chunk], visit, 0)
    out = acc_ref[...] / sum_ref[...]
    out_ref[0] = out
    for h in range(rows // BLK):
        low_out_ref[:, h * head_dim : (h + 1) * head_dim] = (
            jnp.transpose(out[:, h * BLK : (h + 1) * BLK]) + bias_ref[...]
        ).astype(BF16)
    log_ref[0] = top_ref[...] + jnp.log2(sum_ref[...])


def backward_kernel(
    low_ref, high_ref, me_ref, q_ref, grad_ref, out_ref, log_ref, kv_ref, gq_ref, gk_mine, gk_theirs, gv_mine, gv_theirs,
    gk_acc, gv_acc, gq_acc,
    *, head_dim, per_col, per_block, span
):
    chunk = pl.program_id(0)

    @pl.when(chunk == 0)
    def _():
        gk_acc[...] = jnp.zeros_like(gk_acc)
        gv_acc[...] = jnp.zeros_like(gv_acc)

    q = stacked_heads(q_ref[...], head_dim)
    grad = stacked_heads(grad_ref[...], head_dim)
    scale = head_dim ** (-0.5)
    log = log_ref[0]
    delta = jnp.sum(out_ref[0] * jnp.transpose(grad.astype(F32)), 0, keepdims=True)
    gq_acc[...] = jnp.zeros_like(gq_acc)

    def visit(kb, carry):
        col, places = key_pieces(kb, me_ref[0], per_col, per_block, kv_ref.shape[0] // 2)
        at = pl.ds(pl.multiple_of(col * span, span), span)
        kv = jnp.concatenate([kv_ref[place, at, :] for place in places], 0)
        keys, vals = kv[:, :head_dim], kv[:, head_dim:]
        scores = dot_last(keys, q) * (scale * LOG2E)
        probs = jnp.exp2(scores - log)
        grad_probs = dot_last(vals, grad)
        grad_scores = (probs * (grad_probs - delta)).astype(BF16)
        gq_acc[...] += dot_first(keys, grad_scores)
        gk = dot_plain(grad_scores, q)
        gv = dot_plain(probs.astype(BF16), grad)
        for t, place in enumerate(places):
            gk_acc[place, at, :] += gk[t * span : (t + 1) * span]
            gv_acc[place, at, :] += gv[t * span : (t + 1) * span]
        return carry

    lax.fori_loop(low_ref[chunk], high_ref[chunk], visit, 0)
    gq = gq_acc[...] * scale
    for h in range(q.shape[0] // BLK):
        gq_ref[:, h * head_dim : (h + 1) * head_dim] = jnp.transpose(
            gq[:, h * BLK : (h + 1) * BLK]
        ).astype(BF16)

    @pl.when(chunk == pl.num_programs(0) - 1)
    def _():
        half = gk_mine.shape[0]
        gk_mine[...] = gk_acc[:half] * scale
        gk_theirs[...] = (gk_acc[half:] * scale).astype(BF16)
        gv_mine[...] = gv_acc[:half]
        gv_theirs[...] = gv_acc[half:].astype(BF16)


def attention_calls(seq_blocks, tokens_col, span, head_dim, query_cols):
    rows, cols = lax.axis_size("row"), lax.axis_size("col")
    per_col, per_block = tokens_col // BLK, BLK // span
    heads = query_cols // head_dim
    me = lax.axis_index("row")
    ends = jnp.cumsum(seq_blocks)
    blocks = lax.axis_index("col") * per_col + jnp.arange(per_col, dtype=jnp.int32)
    owner = jnp.sum((blocks[:, None] >= ends[None, :]).astype(jnp.int32), 1)
    starts = ends - seq_blocks
    low = jnp.sum(
        jnp.where(owner[:, None] == jnp.arange(ends.shape[0])[None, :], starts[None, :], 0), 1
    ).astype(jnp.int32)
    scalars = (low, (blocks + 1).astype(jnp.int32), jnp.full((1,), me, jnp.int32))
    sizes = dict(head_dim=head_dim, per_col=per_col, per_block=per_block, span=span)
    chunk_rows = pl.BlockSpec((BLK, query_cols), lambda c, *_: (c, 0))
    whole_kv = pl.BlockSpec((rows, cols * span, 2 * head_dim), lambda c, *_: (0, 0, 0))
    half_kv = pl.BlockSpec((rows // 2, cols * span, head_dim), lambda c, *_: (0, 0, 0))
    turned = pl.BlockSpec((1, head_dim, heads * BLK), lambda c, *_: (c, 0, 0))
    logs = pl.BlockSpec((1, 1, heads * BLK), lambda c, *_: (c, 0, 0))
    bias = pl.BlockSpec((1, head_dim), lambda c, *_: (0, 0))
    shape = jax.ShapeDtypeStruct

    def forward(queries, key_values, bias_value):
        return pl.pallas_call(
            partial(forward_kernel, **sizes),
            out_shape=(
                shape((per_col, head_dim, heads * BLK), F32),
                shape((per_col, 1, heads * BLK), F32),
                shape((tokens_col, query_cols), BF16),
            ),
            grid_spec=pltpu.PrefetchScalarGridSpec(
                num_scalar_prefetch=3,
                grid=(per_col,),
                in_specs=[chunk_rows, whole_kv, bias],
                out_specs=(turned, logs, chunk_rows),
                scratch_shapes=[
                    pltpu.VMEM((head_dim, heads * BLK), F32),
                    pltpu.VMEM((1, heads * BLK), F32),
                    pltpu.VMEM((1, heads * BLK), F32),
                ],
            ),
            name="attend_forward",
        )(*scalars, queries, key_values, bias_value)

    def backward(queries, grad_low, out, log, key_values):
        return pl.pallas_call(
            partial(backward_kernel, **sizes),
            out_shape=(
                shape((tokens_col, query_cols), BF16),
                shape((rows // 2, cols * span, head_dim), F32),
                shape((rows // 2, cols * span, head_dim), BF16),
                shape((rows // 2, cols * span, head_dim), F32),
                shape((rows // 2, cols * span, head_dim), BF16),
            ),
            grid_spec=pltpu.PrefetchScalarGridSpec(
                num_scalar_prefetch=3,
                grid=(per_col,),
                in_specs=[chunk_rows, chunk_rows, turned, logs, whole_kv],
                out_specs=(chunk_rows, half_kv, half_kv, half_kv, half_kv),
                scratch_shapes=[
                    pltpu.VMEM((rows, cols * span, head_dim), F32),
                    pltpu.VMEM((rows, cols * span, head_dim), F32),
                    pltpu.VMEM((head_dim, heads * BLK), F32),
                ],
            ),
            name="attend_backward",
        )(*scalars, queries, grad_low, out, log, key_values)

    return forward, backward


def norm_forward(values):
    mean = jnp.mean(values, 1, keepdims=True)
    centred = values - mean
    scale = lax.rsqrt(jnp.mean(centred * centred, 1, keepdims=True) + EPSILON)
    return centred * scale, scale


def norm_backward(grad_out, normed, scale, gain):
    grad_normed = grad_out * gain
    plain = jnp.mean(grad_normed, 1, keepdims=True)
    cross = jnp.mean(grad_normed * normed, 1, keepdims=True)
    grad_in = scale * (grad_normed - plain - normed * cross)
    return grad_in, jnp.sum(grad_out * normed, 0), jnp.sum(grad_out, 0)


def body(
    inputs,
    cotangent,
    seq_blocks,
    first_gain,
    first_shift,
    w_query,
    b_query,
    w_keyval,
    b_value,
    w_out,
    b_out,
    second_gain,
    second_shift,
    w_up,
    b_up,
    w_down,
    b_down,
):
    rows, cols = lax.axis_size("row"), lax.axis_size("col")
    row, col = lax.axis_index("row"), lax.axis_index("col")
    tokens_col, features = inputs.shape
    width = features * rows
    span = tokens_col // rows
    head_dim = b_value.shape[0]
    kv_cols = w_keyval.shape[1]
    head_cols = w_query.shape[1]
    query_cols = head_cols * cols // rows
    heads_each = head_cols // query_cols

    up_cols = w_up.shape[1]

    vectors = jnp.stack([first_gain, first_shift, b_out, second_gain, second_shift, b_down])
    vectors = in_parts(padded(vectors, 8), 3).reshape(24, features)
    steps_x = row_gather(jnp.concatenate([inputs, padded(vectors, 32)], 0))
    fly_x = next(steps_x)
    kv_local = w_keyval.reshape(-1, query_cols)
    local_rows = kv_local.shape[0]
    bias_local = in_parts(b_query.reshape(heads_each, query_cols), 3).reshape(-1, query_cols)
    bias_rows = bias_local.shape[0]
    kv_local = jnp.concatenate([kv_local, padded(bias_local, 16)], 0)
    fly_kv = col_parts(kv_local)
    query_local = jnp.transpose(w_query.reshape(features, heads_each, query_cols), (1, 0, 2))
    fly_x, fly_kv, query_local, w_up_late, w_out_late = barrier(
        fly_x, fly_kv, query_local, w_up, w_out
    )

    w_up_all = lax.all_gather(w_up_late, "row", axis=0, tiled=True)
    fly_q = col_parts(query_local)
    fly_out = col_parts(w_out_late)
    fly_x = advance(steps_x, fly_x)
    kv_join = col_join(kv_local, fly_kv)
    kv_strip = jnp.transpose(
        kv_join[:, :local_rows].reshape(cols, features, kv_cols), (1, 0, 2)
    ).reshape(features, cols * kv_cols)
    bias_parts = lax.dynamic_index_in_dim(
        kv_join[:, local_rows : local_rows + bias_rows], row // heads_each, 0, keepdims=False
    ).reshape(3, heads_each, query_cols)
    bias_query = jnp.sum(
        lax.dynamic_index_in_dim(bias_parts, row % heads_each, 1, keepdims=True).astype(F32), 0
    )
    steps_kv = row_gather(kv_strip)
    fly_kv = next(steps_kv)
    fly_x, fly_kv, fly_q = barrier(fly_x, fly_kv, fly_q)

    query_flat = col_join(query_local, fly_q).reshape(rows, features, query_cols)
    w_query_row = exchange_rows(query_flat)
    fly_x = advance(steps_x, fly_x)
    fly_kv = advance(steps_kv, fly_kv)
    fly_x, fly_kv = barrier(fly_x, fly_kv)

    fly_kv = advance(steps_kv, fly_kv)
    mine, theirs = finish(steps_x, fly_x)
    first_all, own_low, vectors = norm_gathered(mine, theirs, tokens_col, span)
    gain1, shift1, bias_out, gain2, shift2, bias_down = (vectors[k : k + 1] for k in range(6))
    first_all, own_low, fly_kv, w_query_row, cot_late = barrier(
        first_all, own_low, fly_kv, w_query_row, cotangent
    )

    w_kv_all = in_row_order(jnp.concatenate(finish(steps_kv, fly_kv), 0), 0)
    own = own_low.astype(F32)
    first_low = lax.dynamic_slice_in_dim(first_all, row * span, span, 0)
    kv_own = dot_plain(first_low, w_kv_all).astype(BF16)
    fly_kv = col_parts(kv_own)
    cot_own = lax.all_to_all(cot_late, "row", 0, 1, tiled=True)
    fly_kv, fly_out, cot_own = barrier(fly_kv, fly_out, cot_own)
    w_out_all = lax.all_gather(
        col_join(w_out, fly_out).reshape(cols * head_cols, features), "row", axis=1, tiled=True
    )
    steps_kv = row_gather(col_join(kv_own, fly_kv).reshape(cols * span, -1))
    fly_kv = next(steps_kv)
    queries = (dot_plain(first_all, w_query_row.reshape(width, query_cols)) + bias_query).astype(
        BF16
    )
    kv_all = jnp.concatenate(finish(steps_kv, fly_kv), 0)
    queries, kv_all, w_up_all = barrier(queries, kv_all, w_up_all)
    fly_cot = col_parts(cot_own)
    w_down_late, _ = barrier(w_down, queries)
    w_down_all = lax.all_gather(w_down_late, "row", axis=1, tiled=True)

    attend, attend_back = attention_calls(seq_blocks, tokens_col, span, head_dim, query_cols)
    core_turned, logs, attn_low = attend(queries, kv_all, b_value[None, :])
    attn_own = lax.all_to_all(attn_low, "row", 0, 1, tiled=True)
    attn_own, w_out_all, fly_cot = barrier(attn_own, w_out_all, fly_cot)
    middle = own + dot_plain(attn_own, w_out_all) + bias_out

    normed2, scale2 = norm_forward(middle)
    second_low = (normed2 * gain2 + shift2).astype(BF16)
    fly_second = col_parts(second_low)
    query_strip = jnp.transpose(query_flat, (1, 0, 2)).reshape(features, rows * query_cols)
    query_strip, _ = barrier(query_strip, second_low)
    w_query_all = lax.all_gather(query_strip, "row", axis=0, tiled=True)
    cot_all = col_join(cot_own, fly_cot).reshape(cols * span, width)
    fly_second, cot_all = barrier(fly_second, cot_all)
    second_all = col_join(second_low, fly_second).reshape(cols * span, width)
    pre = dot_plain(second_all, w_up_all) + b_up
    grad_hidden = dot_last(cot_all, w_down_all)
    gelu_value, gelu_back = jax.vjp(partial(jax.nn.gelu, approximate=True), pre)
    hidden = gelu_value.astype(BF16)
    grad_pre = gelu_back(grad_hidden)[0].astype(BF16)
    second_part = dot_last(grad_pre, w_up_all).reshape(cols, span, width).astype(BF16)
    second_part, hidden, grad_pre = barrier(second_part, hidden, grad_pre)
    fly_second = col_send(second_part)
    hidden_late, _ = barrier(hidden, fly_second[1])
    up_part = dot_first(second_all, grad_pre).astype(BF16)
    down_part = dot_first(hidden, cot_all).astype(BF16)
    grad_w_down = lax.psum_scatter(down_part, "row", scatter_dimension=1, tiled=True).astype(F32)
    grad_w_up = lax.psum_scatter(up_part, "row", scatter_dimension=0, tiled=True).astype(F32)
    out_part = dot_plain(hidden_late, w_down_all).astype(BF16)
    fly_second, _, _, out_part = barrier(fly_second, down_part, up_part, out_part)
    fly_block = col_send(out_part.reshape(cols, span, width))

    grad_in2, gain2_part, shift2_part = norm_backward(add_up(fly_second), normed2, scale2, gain2)
    grad_middle = cot_own.astype(F32) + grad_in2
    mid_low = grad_middle.astype(BF16)
    late = {}

    def hold(ready):
        if "grad_attn" in late:
            ready, late["grad_attn"] = barrier(ready, late["grad_attn"])
        return list(ready)

    steps_mid = row_gather(mid_low, hold)
    fly_mid = next(steps_mid)
    grad_attn_own = dot_last(mid_low, w_out_all).astype(BF16)
    fly_mid, grad_attn_own = barrier(fly_mid, grad_attn_own)
    late["grad_attn"] = lax.all_to_all(grad_attn_own, "row", 1, 0, tiled=True)
    fly_mid = advance(steps_mid, fly_mid)
    grad_attn = late.pop("grad_attn")

    grad_queries, key_mine, key_theirs, value_mine, value_theirs = attend_back(
        queries, grad_attn, core_turned, logs, kv_all
    )
    grad_queries, key_theirs, value_theirs, fly_mid, fly_block = barrier(
        grad_queries, key_theirs, value_theirs, fly_mid, fly_block
    )

    queries_own = lax.all_to_all(grad_queries, "row", 0, 1, tiled=True)
    steps_kv = row_scatter([key_mine, value_mine], [key_theirs, value_theirs])
    fly_kv = next(steps_kv)
    fly_mid = advance(steps_mid, fly_mid)
    query_part = dot_first(first_all, grad_queries).astype(BF16)
    query_bias = padded(in_parts(jnp.sum(grad_queries.astype(F32), 0), 2), 16)
    up_bias = in_parts(jnp.sum(grad_pre.astype(F32), 0), 2).reshape(-1, query_cols)
    up_rows = up_bias.shape[0]
    extra = jnp.concatenate([query_bias, padded(up_bias, 16)], 0)
    attn_tokens = attn_low.reshape(rows, span, query_cols)
    apart = [2 * k for k in range(rows // 2)]

    def attn_rows(offset):
        return jnp.concatenate(
            [
                lax.dynamic_index_in_dim(attn_tokens, row ^ (p + offset), 0, keepdims=False)
                for p in apart
            ],
            0,
        )

    attn_mine, attn_theirs = attn_rows(0), attn_rows(1)
    fly_kv, fly_mid, queries_own, attn_mine, attn_theirs = barrier(
        fly_kv, fly_mid, queries_own, attn_mine, attn_theirs
    )
    out_own = (middle + add_up(fly_block) + bias_down).astype(BF16)
    fly_kv = advance(steps_kv, fly_kv)
    mid_mine, mid_theirs = finish(steps_mid, fly_mid)
    out_weights = (
        dot_first(mid_mine.reshape(-1, width), attn_mine)
        + dot_first(mid_theirs.reshape(-1, width), attn_theirs)
    ).astype(BF16)
    pieces = jnp.concatenate(
        [
            jnp.transpose(out_own.reshape(span, rows, features), (1, 0, 2)),
            out_weights.reshape(rows, features, query_cols),
            query_part.reshape(rows, features, query_cols),
            jnp.broadcast_to(extra[None], (rows,) + extra.shape),
        ],
        1,
    )
    kv_group = jnp.concatenate(finish(steps_kv, fly_kv), -1)

    pieces, kv_group = barrier(pieces, kv_group)
    fly_kv = col_send(kv_group.reshape(cols, span, -1))
    sent = exchange_rows(pieces)
    kv_mine = add_up(fly_kv).astype(BF16)
    grad_first = dot_last(queries_own, w_query_all) + dot_last(kv_mine, w_kv_all)
    normed1, scale1 = norm_forward(own)
    grad_in1, gain1_part, shift1_part = norm_backward(grad_first, normed1, scale1, gain1)
    feature_parts = jnp.stack(
        [
            gain1_part,
            shift1_part,
            gain2_part,
            shift2_part,
            jnp.sum(mid_low.astype(F32), 0),
            jnp.sum(cot_own.astype(F32), 0),
        ]
    )
    value_part = jnp.sum(grad_attn_own.astype(F32).reshape(-1, head_dim), 0)
    value_rows = jnp.tile(
        jnp.pad(in_parts(value_part, 2), ((0, 0), (0, features - head_dim))), (1, rows)
    )
    stacked = jnp.concatenate(
        [
            (grad_middle + grad_in1).astype(BF16),
            padded(jnp.concatenate([in_parts(feature_parts, 2).reshape(12, width), value_rows], 0), 16),
        ],
        0,
    )
    stacked, kv_mine, sent = barrier(stacked, kv_mine, sent)
    block_output = sent[:, :span].reshape(tokens_col, features)
    last_row = span + 2 * features + 16
    fly_weights = col_send(
        sent[:, span:last_row].reshape(cols, heads_each, 2 * features + 16, query_cols)
    )
    up_total = total(sent[:, last_row : last_row + up_rows]).reshape(2, up_cols)
    last = lax.all_to_all(stacked, "row", 1, 0, tiled=True).reshape(rows, -1, features)
    steps_kv = row_gather(kv_mine)
    kv_tokens = in_row_order(jnp.concatenate(finish(steps_kv, next(steps_kv)), 0), 0)
    first_mine = lax.dynamic_slice_in_dim(first_all, row * features, features, 1)
    kv_sum = dot_first(kv_tokens, first_mine).reshape(cols, kv_cols, features)
    last, kv_sum, grad_w_down, grad_w_up = barrier(last, kv_sum, grad_w_down, grad_w_up)
    grad_inputs = last[:, :span].reshape(tokens_col, features).astype(F32)
    sums = in_parts(total(last[:, -16:]), 2).reshape(32, features)
    fly_sums = col_send(
        jnp.concatenate(
            [kv_sum.astype(BF16), jnp.broadcast_to(sums[None], (cols, 32, features))], 1
        )
    )
    fly_weights, fly_sums = barrier(fly_weights, fly_sums)
    sums = add_up(fly_sums)
    grad_w_keyval = jnp.transpose(sums[:kv_cols])
    sums = sums[kv_cols : kv_cols + 16] + sums[kv_cols + 16 :]
    by_feature = sums[0:6] + sums[6:12]
    grad_b_value = (sums[12] + sums[13])[:head_dim]

    weights = add_up(fly_weights)
    grad_w_out = jnp.transpose(weights[:, :features], (0, 2, 1)).reshape(head_cols, features)
    grad_w_query = jnp.transpose(weights[:, features : 2 * features], (1, 0, 2)).reshape(
        features, head_cols
    )
    grad_b_query = (weights[:, 2 * features] + weights[:, 2 * features + 1]).reshape(head_cols)
    return (
        block_output,
        grad_inputs,
        by_feature[0],
        by_feature[1],
        grad_w_query,
        grad_b_query,
        grad_w_keyval,
        grad_b_value,
        grad_w_out,
        by_feature[4],
        by_feature[2],
        by_feature[3],
        grad_w_up,
        up_total[0] + up_total[1],
        grad_w_down,
        by_feature[5],
    )


def solution(mesh):
    both, rows, cols = P("col", "row"), P("row"), P("col")
    return jax.shard_map(
        body,
        mesh=mesh,
        in_specs=(
            both, both, P(), rows, rows, P("row", "col"), cols, P("row", "col"), P(), both, rows,
            rows, rows, P("row", "col"), cols, both, rows,
        ),
        out_specs=(
            both, both, rows, rows, P("row", "col"), cols, P("row", "col"), P(), both, rows,
            rows, rows, P("row", "col"), cols, both, rows,
        ),
        check_vma=False,
    )
```

```python
from functools import partial

import jax
import jax.numpy as jnp
from jax import lax
from jax.experimental import pallas as pl
from jax.experimental.pallas import tpu as pltpu
from jax.sharding import PartitionSpec as P

BLK = 256
EPSILON = 1e-05
NEGATIVE = -1e30
LOG2E = 1.4426950408889634
F32 = jnp.float32
BF16 = jnp.bfloat16


def barrier(*values):
    return lax.optimization_barrier(values)


def col_parts(value):
    count = lax.axis_size("col")
    return [
        lax.ppermute(value, "col", [(i, (i + step) % count) for i in range(count)])
        for step in range(1, count)
    ]


def col_join(value, parts):
    count = lax.axis_size("col")
    me = lax.axis_index("col")
    out = jnp.zeros((count,) + value.shape, value.dtype)
    out = lax.dynamic_update_index_in_dim(out, value, me, 0)
    for step, part in enumerate(parts, 1):
        out = lax.dynamic_update_index_in_dim(out, part, lax.rem(me - step + count, count), 0)
    return out


def col_send(pieces):
    count = lax.axis_size("col")
    me = lax.axis_index("col")
    low = pieces.astype(BF16)
    out = [lax.dynamic_index_in_dim(low, me, 0, keepdims=False)]
    for step in range(1, count):
        part = lax.dynamic_index_in_dim(low, lax.rem(me + step, count), 0, keepdims=False)
        out.append(
            lax.ppermute(part, "col", [(i, (i + step) % count) for i in range(count)])
        )
    return out


def add_up(parts):
    return sum(part.astype(F32) for part in parts)


def exchange_rows(pieces):
    return lax.all_to_all(pieces.astype(BF16), "row", 0, 0)


def total(pieces):
    return jnp.sum(pieces.astype(F32), 0)


def swap(value, bit):
    count = lax.axis_size("row")
    return lax.ppermute(value, "row", [(i, i ^ bit) for i in range(count)])


def chip_bits():
    bits = []
    bit = 2
    while bit < lax.axis_size("row"):
        bits.append(bit)
        bit *= 2
    return bits


def row_place(other):
    apart = jnp.bitwise_xor(lax.axis_index("row"), other)
    return (apart & 1) * (lax.axis_size("row") // 2) + (apart >> 1)


def in_row_order(pieces, axis):
    count = pieces.shape[0]
    return jnp.concatenate(
        [
            lax.dynamic_index_in_dim(pieces, row_place(a), 0, keepdims=False)
            for a in range(count)
        ],
        axis,
    )


def row_gather(value, hold=list):
    half = value.shape[-1] // 2
    bits = chip_bits()
    orders = (bits, bits[::-1])
    held = [{0: value[..., :half]}, {0: value[..., half:]}]
    for step in range(len(bits)):
        keys = [sorted(h) for h in held]
        ready = hold([jnp.stack([h[k] for k in ks]) for h, ks in zip(held, keys)])
        got = yield [swap(part, order[step]) for part, order in zip(ready, orders)]
        for h, ks, order, new in zip(held, keys, orders, got):
            h.update({k ^ order[step]: new[n] for n, k in enumerate(ks)})
    own = jnp.stack([jnp.concatenate([held[0][k], held[1][k]], -1) for k in sorted(held[0])])
    (other,) = yield [swap(own, 1)]
    return own, other


def row_scatter(mine, theirs):
    got = yield [swap(part, 1) for part in theirs]
    bits = chip_bits()
    orders = (bits[::-1], bits)
    held = []
    for part, new in zip(mine, got):
        both = part + new.astype(F32)
        held.append({2 * k: both[k] for k in range(both.shape[0])})
    for step in range(len(bits)):
        keeps = [sorted(k for k in h if not k & order[step]) for h, order in zip(held, orders)]
        got = yield [
            swap(jnp.stack([h[k ^ order[step]] for k in keep]).astype(BF16), order[step])
            for h, keep, order in zip(held, keeps, orders)
        ]
        held = [
            {k: h[k] + new[n].astype(F32) for n, k in enumerate(keep)}
            for h, keep, new in zip(held, keeps, got)
        ]
    return [h[0] for h in held]


def advance(steps, arrived):
    try:
        return steps.send(list(arrived))
    except StopIteration as stop:
        return {"done": stop.value}


def finish(steps, arrived):
    while True:
        arrived = advance(steps, list(barrier(*arrived)))
        if isinstance(arrived, dict):
            return arrived["done"]


def in_parts(vector, count):
    parts = []
    for _ in range(count):
        low = lax.reduce_precision(vector, 8, 7)
        parts.append(low.astype(BF16))
        vector = vector - low
    return jnp.stack(parts)


def padded(rows_array, multiple):
    short = -rows_array.shape[0] % multiple
    return jnp.pad(rows_array, ((0, short), (0, 0)))


def norm_kernel(
    me_ref, mine_ref, theirs_ref, mine_vec, theirs_vec, mine_own, theirs_own,
    first_ref, own_ref, vector_ref,
    *, width
):
    half = mine_ref.shape[0]
    features = mine_ref.shape[2]
    places = [(mine_ref, mine_vec, mine_own, 2 * k, k) for k in range(half)]
    places += [(theirs_ref, theirs_vec, theirs_own, 2 * k + 1, k) for k in range(half)]
    me = me_ref[0]

    def columns(apart):
        return pl.ds(pl.multiple_of(jnp.bitwise_xor(me, apart) * features, features), features)

    @pl.when(pl.program_id(0) == 0)
    def _():
        for _, vec, own, apart, k in places:
            stack = vec[k].astype(F32)
            vector_ref[:, columns(apart)] = stack[0:8] + stack[8:16] + stack[16:24]
            own_ref[:, columns(apart)] = own[k]

    sums = sum(jnp.sum(ref[k].astype(F32), 1, keepdims=True) for ref, _, _, _, k in places)
    mean = sums / width
    squares = jnp.zeros_like(mean)
    for ref, _, _, _, k in places:
        centred = ref[k].astype(F32) - mean
        squares = squares + jnp.sum(centred * centred, 1, keepdims=True)
    scale = lax.rsqrt(squares / width + EPSILON)
    for ref, vec, _, apart, k in places:
        stack = vec[k].astype(F32)
        both = stack[0:8] + stack[8:16] + stack[16:24]
        normed = (ref[k].astype(F32) - mean) * scale
        first_ref[:, columns(apart)] = (normed * both[0:1] + both[1:2]).astype(BF16)


def norm_gathered(mine, theirs, tokens, span):
    rows = lax.axis_size("row")
    half, _, features = mine.shape
    width = features * rows
    me = jnp.full((1,), lax.axis_index("row"), jnp.int32)
    block = pl.BlockSpec((half, BLK, features), lambda i, _: (0, i, 0))
    vec = pl.BlockSpec((half, 32, features), lambda i, _: (0, tokens // 32, 0))
    own = pl.BlockSpec((half, span, features), lambda i, m: (0, m[0], 0))
    return pl.pallas_call(
        partial(norm_kernel, width=width),
        out_shape=(
            jax.ShapeDtypeStruct((tokens, width), BF16),
            jax.ShapeDtypeStruct((span, width), BF16),
            jax.ShapeDtypeStruct((8, width), F32),
        ),
        grid_spec=pltpu.PrefetchScalarGridSpec(
            num_scalar_prefetch=1,
            grid=(tokens // BLK,),
            in_specs=[block, block, vec, vec, own, own],
            out_specs=(
                pl.BlockSpec((BLK, width), lambda i, _: (i, 0)),
                pl.BlockSpec((span, width), lambda i, _: (0, 0)),
                pl.BlockSpec((8, width), lambda i, _: (0, 0)),
            ),
        ),
        name="norm_gathered",
    )(me, mine, theirs, mine, theirs, mine, theirs)


def stacked_heads(block, head_dim):
    count = block.shape[1] // head_dim
    return jnp.concatenate([block[:, h * head_dim : (h + 1) * head_dim] for h in range(count)], 0)


def dot_last(left, right):
    return lax.dot_general(left, right, (((1,), (1,)), ((), ())), preferred_element_type=F32)


def dot_first(left, right):
    return lax.dot_general(left, right, (((0,), (0,)), ((), ())), preferred_element_type=F32)


def dot_plain(left, right):
    return lax.dot_general(left, right, (((1,), (0,)), ((), ())), preferred_element_type=F32)


def key_pieces(kb, me, per_col, per_block, half):
    col = lax.div(kb, per_col)
    first = lax.rem(kb, per_col) * per_block
    places = []
    for t in range(per_block):
        apart = jnp.bitwise_xor(first + t, me)
        places.append((apart & 1) * half + lax.shift_right_logical(apart, 1))
    return col, places


def forward_kernel(
    low_ref, high_ref, me_ref, q_ref, kv_ref, bias_ref, out_ref, log_ref, low_out_ref, acc_ref, top_ref, sum_ref,
    *, head_dim, per_col, per_block, span
):
    chunk = pl.program_id(0)
    q = stacked_heads(q_ref[...], head_dim)
    rows = q.shape[0]
    acc_ref[...] = jnp.zeros_like(acc_ref)
    top_ref[...] = jnp.full_like(top_ref, NEGATIVE)
    sum_ref[...] = jnp.zeros_like(sum_ref)
    factor = head_dim ** (-0.5) * LOG2E

    def visit(kb, carry):
        col, places = key_pieces(kb, me_ref[0], per_col, per_block, kv_ref.shape[0] // 2)
        at = pl.ds(pl.multiple_of(col * span, span), span)
        kv = jnp.concatenate([kv_ref[place, at, :] for place in places], 0)
        scores = dot_last(kv[:, :head_dim], q) * factor
        old = top_ref[...]
        new = jnp.maximum(old, jnp.max(scores, 0, keepdims=True))
        weights = jnp.exp2(scores - new)
        decay = jnp.exp2(old - new)
        top_ref[...] = new
        sum_ref[...] = sum_ref[...] * decay + jnp.sum(weights, 0, keepdims=True)
        acc_ref[...] = acc_ref[...] * decay + dot_first(kv[:, head_dim:], weights.astype(BF16))
        return carry

    lax.fori_loop(low_ref[chunk], high_ref[chunk], visit, 0)
    out = acc_ref[...] / sum_ref[...]
    out_ref[0] = out
    for h in range(rows // BLK):
        low_out_ref[:, h * head_dim : (h + 1) * head_dim] = (
            jnp.transpose(out[:, h * BLK : (h + 1) * BLK]) + bias_ref[...]
        ).astype(BF16)
    log_ref[0] = top_ref[...] + jnp.log2(sum_ref[...])


def backward_kernel(
    low_ref, high_ref, me_ref, q_ref, grad_ref, out_ref, log_ref, kv_ref, gq_ref, gk_mine, gk_theirs, gv_mine, gv_theirs,
    gk_acc, gv_acc, gq_acc,
    *, head_dim, per_col, per_block, span
):
    chunk = pl.program_id(0)

    @pl.when(chunk == 0)
    def _():
        gk_acc[...] = jnp.zeros_like(gk_acc)
        gv_acc[...] = jnp.zeros_like(gv_acc)

    q = stacked_heads(q_ref[...], head_dim)
    grad = stacked_heads(grad_ref[...], head_dim)
    scale = head_dim ** (-0.5)
    log = log_ref[0]
    delta = jnp.sum(out_ref[0] * jnp.transpose(grad.astype(F32)), 0, keepdims=True)
    gq_acc[...] = jnp.zeros_like(gq_acc)

    def visit(kb, carry):
        col, places = key_pieces(kb, me_ref[0], per_col, per_block, kv_ref.shape[0] // 2)
        at = pl.ds(pl.multiple_of(col * span, span), span)
        kv = jnp.concatenate([kv_ref[place, at, :] for place in places], 0)
        keys, vals = kv[:, :head_dim], kv[:, head_dim:]
        scores = dot_last(keys, q) * (scale * LOG2E)
        probs = jnp.exp2(scores - log)
        grad_probs = dot_last(vals, grad)
        grad_scores = (probs * (grad_probs - delta)).astype(BF16)
        gq_acc[...] += dot_first(keys, grad_scores)
        gk = dot_plain(grad_scores, q)
        gv = dot_plain(probs.astype(BF16), grad)
        for t, place in enumerate(places):
            gk_acc[place, at, :] += gk[t * span : (t + 1) * span]
            gv_acc[place, at, :] += gv[t * span : (t + 1) * span]
        return carry

    lax.fori_loop(low_ref[chunk], high_ref[chunk], visit, 0)
    gq = gq_acc[...] * scale
    for h in range(q.shape[0] // BLK):
        gq_ref[:, h * head_dim : (h + 1) * head_dim] = jnp.transpose(
            gq[:, h * BLK : (h + 1) * BLK]
        ).astype(BF16)

    @pl.when(chunk == pl.num_programs(0) - 1)
    def _():
        half = gk_mine.shape[0]
        gk_mine[...] = gk_acc[:half] * scale
        gk_theirs[...] = (gk_acc[half:] * scale).astype(BF16)
        gv_mine[...] = gv_acc[:half]
        gv_theirs[...] = gv_acc[half:].astype(BF16)


def attention_calls(seq_blocks, tokens_col, span, head_dim, query_cols):
    rows, cols = lax.axis_size("row"), lax.axis_size("col")
    per_col, per_block = tokens_col // BLK, BLK // span
    heads = query_cols // head_dim
    me = lax.axis_index("row")
    ends = jnp.cumsum(seq_blocks)
    blocks = lax.axis_index("col") * per_col + jnp.arange(per_col, dtype=jnp.int32)
    owner = jnp.sum((blocks[:, None] >= ends[None, :]).astype(jnp.int32), 1)
    starts = ends - seq_blocks
    low = jnp.sum(
        jnp.where(owner[:, None] == jnp.arange(ends.shape[0])[None, :], starts[None, :], 0), 1
    ).astype(jnp.int32)
    scalars = (low, (blocks + 1).astype(jnp.int32), jnp.full((1,), me, jnp.int32))
    sizes = dict(head_dim=head_dim, per_col=per_col, per_block=per_block, span=span)
    chunk_rows = pl.BlockSpec((BLK, query_cols), lambda c, *_: (c, 0))
    whole_kv = pl.BlockSpec((rows, cols * span, 2 * head_dim), lambda c, *_: (0, 0, 0))
    half_kv = pl.BlockSpec((rows // 2, cols * span, head_dim), lambda c, *_: (0, 0, 0))
    turned = pl.BlockSpec((1, head_dim, heads * BLK), lambda c, *_: (c, 0, 0))
    logs = pl.BlockSpec((1, 1, heads * BLK), lambda c, *_: (c, 0, 0))
    bias = pl.BlockSpec((1, head_dim), lambda c, *_: (0, 0))
    shape = jax.ShapeDtypeStruct

    def forward(queries, key_values, bias_value):
        return pl.pallas_call(
            partial(forward_kernel, **sizes),
            out_shape=(
                shape((per_col, head_dim, heads * BLK), F32),
                shape((per_col, 1, heads * BLK), F32),
                shape((tokens_col, query_cols), BF16),
            ),
            grid_spec=pltpu.PrefetchScalarGridSpec(
                num_scalar_prefetch=3,
                grid=(per_col,),
                in_specs=[chunk_rows, whole_kv, bias],
                out_specs=(turned, logs, chunk_rows),
                scratch_shapes=[
                    pltpu.VMEM((head_dim, heads * BLK), F32),
                    pltpu.VMEM((1, heads * BLK), F32),
                    pltpu.VMEM((1, heads * BLK), F32),
                ],
            ),
            name="attend_forward",
        )(*scalars, queries, key_values, bias_value)

    def backward(queries, grad_low, out, log, key_values):
        return pl.pallas_call(
            partial(backward_kernel, **sizes),
            out_shape=(
                shape((tokens_col, query_cols), BF16),
                shape((rows // 2, cols * span, head_dim), F32),
                shape((rows // 2, cols * span, head_dim), BF16),
                shape((rows // 2, cols * span, head_dim), F32),
                shape((rows // 2, cols * span, head_dim), BF16),
            ),
            grid_spec=pltpu.PrefetchScalarGridSpec(
                num_scalar_prefetch=3,
                grid=(per_col,),
                in_specs=[chunk_rows, chunk_rows, turned, logs, whole_kv],
                out_specs=(chunk_rows, half_kv, half_kv, half_kv, half_kv),
                scratch_shapes=[
                    pltpu.VMEM((rows, cols * span, head_dim), F32),
                    pltpu.VMEM((rows, cols * span, head_dim), F32),
                    pltpu.VMEM((head_dim, heads * BLK), F32),
                ],
            ),
            name="attend_backward",
        )(*scalars, queries, grad_low, out, log, key_values)

    return forward, backward


def norm_forward(values):
    mean = jnp.mean(values, 1, keepdims=True)
    centred = values - mean
    scale = lax.rsqrt(jnp.mean(centred * centred, 1, keepdims=True) + EPSILON)
    return centred * scale, scale


def norm_backward(grad_out, normed, scale, gain):
    grad_normed = grad_out * gain
    plain = jnp.mean(grad_normed, 1, keepdims=True)
    cross = jnp.mean(grad_normed * normed, 1, keepdims=True)
    grad_in = scale * (grad_normed - plain - normed * cross)
    return grad_in, jnp.sum(grad_out * normed, 0), jnp.sum(grad_out, 0)


def body(
    inputs,
    cotangent,
    seq_blocks,
    first_gain,
    first_shift,
    w_query,
    b_query,
    w_keyval,
    b_value,
    w_out,
    b_out,
    second_gain,
    second_shift,
    w_up,
    b_up,
    w_down,
    b_down,
):
    rows, cols = lax.axis_size("row"), lax.axis_size("col")
    row, col = lax.axis_index("row"), lax.axis_index("col")
    tokens_col, features = inputs.shape
    width = features * rows
    span = tokens_col // rows
    head_dim = b_value.shape[0]
    kv_cols = w_keyval.shape[1]
    head_cols = w_query.shape[1]
    query_cols = head_cols * cols // rows
    heads_each = head_cols // query_cols

    up_cols = w_up.shape[1]

    vectors = jnp.stack([first_gain, first_shift, b_out, second_gain, second_shift, b_down])
    vectors = in_parts(padded(vectors, 8), 3).reshape(24, features)
    steps_x = row_gather(jnp.concatenate([inputs, padded(vectors, 32)], 0))
    fly_x = next(steps_x)
    kv_local = w_keyval.reshape(-1, query_cols)
    local_rows = kv_local.shape[0]
    bias_local = in_parts(b_query.reshape(heads_each, query_cols), 3).reshape(-1, query_cols)
    bias_rows = bias_local.shape[0]
    kv_local = jnp.concatenate([kv_local, padded(bias_local, 16)], 0)
    fly_kv = col_parts(kv_local)
    query_local = jnp.transpose(w_query.reshape(features, heads_each, query_cols), (1, 0, 2))
    fly_x, fly_kv, query_local, w_out_late = barrier(fly_x, fly_kv, query_local, w_out)

    fly_q = col_parts(query_local)
    fly_out = col_parts(w_out_late)
    fly_x = advance(steps_x, fly_x)
    kv_join = col_join(kv_local, fly_kv)
    kv_strip = jnp.transpose(
        kv_join[:, :local_rows].reshape(cols, features, kv_cols), (1, 0, 2)
    ).reshape(features, cols * kv_cols)
    bias_parts = lax.dynamic_index_in_dim(
        kv_join[:, local_rows : local_rows + bias_rows], row // heads_each, 0, keepdims=False
    ).reshape(3, heads_each, query_cols)
    bias_query = jnp.sum(
        lax.dynamic_index_in_dim(bias_parts, row % heads_each, 1, keepdims=True).astype(F32), 0
    )
    steps_kv = row_gather(kv_strip)
    fly_kv = next(steps_kv)
    fly_x, fly_kv, fly_q, w_up_late = barrier(fly_x, fly_kv, fly_q, w_up)

    w_up_all = lax.all_gather(w_up_late, "row", axis=0, tiled=True)
    query_flat = col_join(query_local, fly_q).reshape(rows, features, query_cols)
    w_query_row = exchange_rows(query_flat)
    fly_x = advance(steps_x, fly_x)
    fly_kv = advance(steps_kv, fly_kv)
    fly_x, fly_kv = barrier(fly_x, fly_kv)

    fly_kv = advance(steps_kv, fly_kv)
    mine, theirs = finish(steps_x, fly_x)
    first_all, own_low, vectors = norm_gathered(mine, theirs, tokens_col, span)
    gain1, shift1, bias_out, gain2, shift2, bias_down = (vectors[k : k + 1] for k in range(6))
    first_all, own_low, fly_kv, w_query_row, cot_late = barrier(
        first_all, own_low, fly_kv, w_query_row, cotangent
    )

    w_kv_all = in_row_order(jnp.concatenate(finish(steps_kv, fly_kv), 0), 0)
    own = own_low.astype(F32)
    first_low = lax.dynamic_slice_in_dim(first_all, row * span, span, 0)
    kv_own = dot_plain(first_low, w_kv_all).astype(BF16)
    fly_kv = col_parts(kv_own)
    cot_own = lax.all_to_all(cot_late, "row", 0, 1, tiled=True)
    fly_kv, fly_out, cot_own = barrier(fly_kv, fly_out, cot_own)
    w_out_all = lax.all_gather(
        col_join(w_out, fly_out).reshape(cols * head_cols, features), "row", axis=1, tiled=True
    )
    steps_kv = row_gather(col_join(kv_own, fly_kv).reshape(cols * span, -1))
    fly_kv = next(steps_kv)
    queries = (dot_plain(first_all, w_query_row.reshape(width, query_cols)) + bias_query).astype(
        BF16
    )
    kv_all = jnp.concatenate(finish(steps_kv, fly_kv), 0)
    queries, kv_all, w_up_all = barrier(queries, kv_all, w_up_all)
    fly_cot = col_parts(cot_own)
    w_down_late, _ = barrier(w_down, queries)
    w_down_all = lax.all_gather(w_down_late, "row", axis=1, tiled=True)

    attend, attend_back = attention_calls(seq_blocks, tokens_col, span, head_dim, query_cols)
    core_turned, logs, attn_low = attend(queries, kv_all, b_value[None, :])
    attn_own = lax.all_to_all(attn_low, "row", 0, 1, tiled=True)
    attn_own, w_out_all, fly_cot = barrier(attn_own, w_out_all, fly_cot)
    middle = own + dot_plain(attn_own, w_out_all) + bias_out

    normed2, scale2 = norm_forward(middle)
    second_low = (normed2 * gain2 + shift2).astype(BF16)
    fly_second = col_parts(second_low)
    query_strip = jnp.transpose(query_flat, (1, 0, 2)).reshape(features, rows * query_cols)
    query_strip, _ = barrier(query_strip, second_low)
    w_query_all = lax.all_gather(query_strip, "row", axis=0, tiled=True)
    cot_all = col_join(cot_own, fly_cot).reshape(cols * span, width)
    fly_second, cot_all = barrier(fly_second, cot_all)
    second_all = col_join(second_low, fly_second).reshape(cols * span, width)
    pre = dot_plain(second_all, w_up_all) + b_up
    grad_hidden = dot_last(cot_all, w_down_all)
    gelu_value, gelu_back = jax.vjp(partial(jax.nn.gelu, approximate=True), pre)
    hidden = gelu_value.astype(BF16)
    grad_pre = gelu_back(grad_hidden)[0].astype(BF16)
    second_part = dot_last(grad_pre, w_up_all).reshape(cols, span, width).astype(BF16)
    second_part, hidden, grad_pre = barrier(second_part, hidden, grad_pre)
    fly_second = col_send(second_part)
    hidden_late, _ = barrier(hidden, fly_second[1])
    up_part = dot_first(second_all, grad_pre).astype(BF16)
    down_part = dot_first(hidden, cot_all).astype(BF16)
    grad_w_down = lax.psum_scatter(down_part, "row", scatter_dimension=1, tiled=True).astype(F32)
    grad_w_up = lax.psum_scatter(up_part, "row", scatter_dimension=0, tiled=True).astype(F32)
    out_part = dot_plain(hidden_late, w_down_all).astype(BF16)
    fly_second, _, _, out_part = barrier(fly_second, down_part, up_part, out_part)
    fly_block = col_send(out_part.reshape(cols, span, width))

    grad_in2, gain2_part, shift2_part = norm_backward(add_up(fly_second), normed2, scale2, gain2)
    grad_middle = cot_own.astype(F32) + grad_in2
    mid_low = grad_middle.astype(BF16)
    late = {}

    def hold(ready):
        if "grad_attn" in late:
            ready, late["grad_attn"] = barrier(ready, late["grad_attn"])
        return list(ready)

    steps_mid = row_gather(mid_low, hold)
    fly_mid = next(steps_mid)
    grad_attn_own = dot_last(mid_low, w_out_all).astype(BF16)
    fly_mid, grad_attn_own = barrier(fly_mid, grad_attn_own)
    late["grad_attn"] = lax.all_to_all(grad_attn_own, "row", 1, 0, tiled=True)
    fly_mid = advance(steps_mid, fly_mid)
    grad_attn = late.pop("grad_attn")

    grad_queries, key_mine, key_theirs, value_mine, value_theirs = attend_back(
        queries, grad_attn, core_turned, logs, kv_all
    )
    grad_queries, key_theirs, value_theirs, fly_mid, fly_block = barrier(
        grad_queries, key_theirs, value_theirs, fly_mid, fly_block
    )

    queries_own = lax.all_to_all(grad_queries, "row", 0, 1, tiled=True)
    steps_kv = row_scatter([key_mine, value_mine], [key_theirs, value_theirs])
    fly_kv = next(steps_kv)
    fly_mid = advance(steps_mid, fly_mid)
    query_part = dot_first(first_all, grad_queries).astype(BF16)
    query_bias = padded(in_parts(jnp.sum(grad_queries.astype(F32), 0), 2), 16)
    up_bias = in_parts(jnp.sum(grad_pre.astype(F32), 0), 2).reshape(-1, query_cols)
    up_rows = up_bias.shape[0]
    extra = jnp.concatenate([query_bias, padded(up_bias, 16)], 0)
    attn_tokens = attn_low.reshape(rows, span, query_cols)
    apart = [2 * k for k in range(rows // 2)]

    def attn_rows(offset):
        return jnp.concatenate(
            [
                lax.dynamic_index_in_dim(attn_tokens, row ^ (p + offset), 0, keepdims=False)
                for p in apart
            ],
            0,
        )

    attn_mine, attn_theirs = attn_rows(0), attn_rows(1)
    fly_kv, fly_mid, queries_own, attn_mine, attn_theirs = barrier(
        fly_kv, fly_mid, queries_own, attn_mine, attn_theirs
    )
    out_own = (middle + add_up(fly_block) + bias_down).astype(BF16)
    fly_kv = advance(steps_kv, fly_kv)
    mid_mine, mid_theirs = finish(steps_mid, fly_mid)
    out_weights = (
        dot_first(mid_mine.reshape(-1, width), attn_mine)
        + dot_first(mid_theirs.reshape(-1, width), attn_theirs)
    ).astype(BF16)
    pieces = jnp.concatenate(
        [
            jnp.transpose(out_own.reshape(span, rows, features), (1, 0, 2)),
            out_weights.reshape(rows, features, query_cols),
            query_part.reshape(rows, features, query_cols),
            jnp.broadcast_to(extra[None], (rows,) + extra.shape),
        ],
        1,
    )
    kv_group = jnp.concatenate(finish(steps_kv, fly_kv), -1)

    pieces, kv_group = barrier(pieces, kv_group)
    fly_kv = col_send(kv_group.reshape(cols, span, -1))
    sent = exchange_rows(pieces)
    kv_mine = add_up(fly_kv).astype(BF16)
    grad_first = dot_last(queries_own, w_query_all) + dot_last(kv_mine, w_kv_all)
    normed1, scale1 = norm_forward(own)
    grad_in1, gain1_part, shift1_part = norm_backward(grad_first, normed1, scale1, gain1)
    feature_parts = jnp.stack(
        [
            gain1_part,
            shift1_part,
            gain2_part,
            shift2_part,
            jnp.sum(mid_low.astype(F32), 0),
            jnp.sum(cot_own.astype(F32), 0),
        ]
    )
    value_part = jnp.sum(grad_attn_own.astype(F32).reshape(-1, head_dim), 0)
    value_rows = jnp.tile(
        jnp.pad(in_parts(value_part, 2), ((0, 0), (0, features - head_dim))), (1, rows)
    )
    stacked = jnp.concatenate(
        [
            (grad_middle + grad_in1).astype(BF16),
            padded(jnp.concatenate([in_parts(feature_parts, 2).reshape(12, width), value_rows], 0), 16),
        ],
        0,
    )
    stacked, kv_mine, sent = barrier(stacked, kv_mine, sent)
    block_output = sent[:, :span].reshape(tokens_col, features)
    last_row = span + 2 * features + 16
    fly_weights = col_send(
        sent[:, span:last_row].reshape(cols, heads_each, 2 * features + 16, query_cols)
    )
    up_total = total(sent[:, last_row : last_row + up_rows]).reshape(2, up_cols)
    last = lax.all_to_all(stacked, "row", 1, 0, tiled=True).reshape(rows, -1, features)
    steps_kv = row_gather(kv_mine)
    kv_tokens = in_row_order(jnp.concatenate(finish(steps_kv, next(steps_kv)), 0), 0)
    first_mine = lax.dynamic_slice_in_dim(first_all, row * features, features, 1)
    kv_sum = dot_first(kv_tokens, first_mine).reshape(cols, kv_cols, features)
    last, kv_sum, grad_w_down, grad_w_up = barrier(last, kv_sum, grad_w_down, grad_w_up)
    grad_inputs = last[:, :span].reshape(tokens_col, features).astype(F32)
    sums = in_parts(total(last[:, -16:]), 2).reshape(32, features)
    fly_sums = col_send(
        jnp.concatenate(
            [kv_sum.astype(BF16), jnp.broadcast_to(sums[None], (cols, 32, features))], 1
        )
    )
    fly_weights, fly_sums = barrier(fly_weights, fly_sums)
    sums = add_up(fly_sums)
    grad_w_keyval = jnp.transpose(sums[:kv_cols])
    sums = sums[kv_cols : kv_cols + 16] + sums[kv_cols + 16 :]
    by_feature = sums[0:6] + sums[6:12]
    grad_b_value = (sums[12] + sums[13])[:head_dim]

    weights = add_up(fly_weights)
    grad_w_out = jnp.transpose(weights[:, :features], (0, 2, 1)).reshape(head_cols, features)
    grad_w_query = jnp.transpose(weights[:, features : 2 * features], (1, 0, 2)).reshape(
        features, head_cols
    )
    grad_b_query = (weights[:, 2 * features] + weights[:, 2 * features + 1]).reshape(head_cols)
    return (
        block_output,
        grad_inputs,
        by_feature[0],
        by_feature[1],
        grad_w_query,
        grad_b_query,
        grad_w_keyval,
        grad_b_value,
        grad_w_out,
        by_feature[4],
        by_feature[2],
        by_feature[3],
        grad_w_up,
        up_total[0] + up_total[1],
        grad_w_down,
        by_feature[5],
    )


def solution(mesh):
    both, rows, cols = P("col", "row"), P("row"), P("col")
    return jax.shard_map(
        body,
        mesh=mesh,
        in_specs=(
            both, both, P(), rows, rows, P("row", "col"), cols, P("row", "col"), P(), both, rows,
            rows, rows, P("row", "col"), cols, both, rows,
        ),
        out_specs=(
            both, both, rows, rows, P("row", "col"), cols, P("row", "col"), P(), both, rows,
            rows, rows, P("row", "col"), cols, both, rows,
        ),
        check_vma=False,
    )
```

```python
from functools import partial

import jax
import jax.numpy as jnp
from jax import lax
from jax.experimental import pallas as pl
from jax.experimental.pallas import tpu as pltpu
from jax.sharding import PartitionSpec as P

BLK = 256
EPSILON = 1e-05
NEGATIVE = -1e30
LOG2E = 1.4426950408889634
F32 = jnp.float32
BF16 = jnp.bfloat16


def barrier(*values):
    return lax.optimization_barrier(values)


def col_parts(value):
    count = lax.axis_size("col")
    return [
        lax.ppermute(value, "col", [(i, (i + step) % count) for i in range(count)])
        for step in range(1, count)
    ]


def col_join(value, parts):
    count = lax.axis_size("col")
    me = lax.axis_index("col")
    out = jnp.zeros((count,) + value.shape, value.dtype)
    out = lax.dynamic_update_index_in_dim(out, value, me, 0)
    for step, part in enumerate(parts, 1):
        out = lax.dynamic_update_index_in_dim(out, part, lax.rem(me - step + count, count), 0)
    return out


def col_send(pieces):
    count = lax.axis_size("col")
    me = lax.axis_index("col")
    low = pieces.astype(BF16)
    out = [lax.dynamic_index_in_dim(low, me, 0, keepdims=False)]
    for step in range(1, count):
        part = lax.dynamic_index_in_dim(low, lax.rem(me + step, count), 0, keepdims=False)
        out.append(
            lax.ppermute(part, "col", [(i, (i + step) % count) for i in range(count)])
        )
    return out


def add_up(parts):
    return sum(part.astype(F32) for part in parts)


def exchange_rows(pieces):
    return lax.all_to_all(pieces.astype(BF16), "row", 0, 0)


def total(pieces):
    return jnp.sum(pieces.astype(F32), 0)


def swap(value, bit):
    count = lax.axis_size("row")
    return lax.ppermute(value, "row", [(i, i ^ bit) for i in range(count)])


def chip_bits():
    bits = []
    bit = 2
    while bit < lax.axis_size("row"):
        bits.append(bit)
        bit *= 2
    return bits


def row_place(other):
    apart = jnp.bitwise_xor(lax.axis_index("row"), other)
    return (apart & 1) * (lax.axis_size("row") // 2) + (apart >> 1)


def in_row_order(pieces, axis):
    count = pieces.shape[0]
    return jnp.concatenate(
        [
            lax.dynamic_index_in_dim(pieces, row_place(a), 0, keepdims=False)
            for a in range(count)
        ],
        axis,
    )


def row_gather(value, hold=list):
    half = value.shape[-1] // 2
    bits = chip_bits()
    orders = (bits, bits[::-1])
    held = [{0: value[..., :half]}, {0: value[..., half:]}]
    for step in range(len(bits)):
        keys = [sorted(h) for h in held]
        ready = hold([jnp.stack([h[k] for k in ks]) for h, ks in zip(held, keys)])
        got = yield [swap(part, order[step]) for part, order in zip(ready, orders)]
        for h, ks, order, new in zip(held, keys, orders, got):
            h.update({k ^ order[step]: new[n] for n, k in enumerate(ks)})
    own = jnp.stack([jnp.concatenate([held[0][k], held[1][k]], -1) for k in sorted(held[0])])
    (other,) = yield [swap(own, 1)]
    return own, other


def row_scatter(mine, theirs):
    got = yield [swap(part, 1) for part in theirs]
    bits = chip_bits()
    orders = (bits[::-1], bits)
    held = []
    for part, new in zip(mine, got):
        both = part + new.astype(F32)
        held.append({2 * k: both[k] for k in range(both.shape[0])})
    for step in range(len(bits)):
        keeps = [sorted(k for k in h if not k & order[step]) for h, order in zip(held, orders)]
        got = yield [
            swap(jnp.stack([h[k ^ order[step]] for k in keep]).astype(BF16), order[step])
            for h, keep, order in zip(held, keeps, orders)
        ]
        held = [
            {k: h[k] + new[n].astype(F32) for n, k in enumerate(keep)}
            for h, keep, new in zip(held, keeps, got)
        ]
    return [h[0] for h in held]


def advance(steps, arrived):
    try:
        return steps.send(list(arrived))
    except StopIteration as stop:
        return {"done": stop.value}


def finish(steps, arrived):
    while True:
        arrived = advance(steps, list(barrier(*arrived)))
        if isinstance(arrived, dict):
            return arrived["done"]


def in_parts(vector, count):
    parts = []
    for _ in range(count):
        low = lax.reduce_precision(vector, 8, 7)
        parts.append(low.astype(BF16))
        vector = vector - low
    return jnp.stack(parts)


def padded(rows_array, multiple):
    short = -rows_array.shape[0] % multiple
    return jnp.pad(rows_array, ((0, short), (0, 0)))


def norm_kernel(
    me_ref, mine_ref, theirs_ref, mine_vec, theirs_vec, mine_own, theirs_own,
    first_ref, own_ref, vector_ref,
    *, width
):
    half = mine_ref.shape[0]
    features = mine_ref.shape[2]
    places = [(mine_ref, mine_vec, mine_own, 2 * k, k) for k in range(half)]
    places += [(theirs_ref, theirs_vec, theirs_own, 2 * k + 1, k) for k in range(half)]
    me = me_ref[0]

    def columns(apart):
        return pl.ds(pl.multiple_of(jnp.bitwise_xor(me, apart) * features, features), features)

    @pl.when(pl.program_id(0) == 0)
    def _():
        for _, vec, own, apart, k in places:
            stack = vec[k].astype(F32)
            vector_ref[:, columns(apart)] = stack[0:8] + stack[8:16] + stack[16:24]
            own_ref[:, columns(apart)] = own[k]

    sums = sum(jnp.sum(ref[k].astype(F32), 1, keepdims=True) for ref, _, _, _, k in places)
    mean = sums / width
    squares = jnp.zeros_like(mean)
    for ref, _, _, _, k in places:
        centred = ref[k].astype(F32) - mean
        squares = squares + jnp.sum(centred * centred, 1, keepdims=True)
    scale = lax.rsqrt(squares / width + EPSILON)
    for ref, vec, _, apart, k in places:
        stack = vec[k].astype(F32)
        both = stack[0:8] + stack[8:16] + stack[16:24]
        normed = (ref[k].astype(F32) - mean) * scale
        first_ref[:, columns(apart)] = (normed * both[0:1] + both[1:2]).astype(BF16)


def norm_gathered(mine, theirs, tokens, span):
    rows = lax.axis_size("row")
    half, _, features = mine.shape
    width = features * rows
    me = jnp.full((1,), lax.axis_index("row"), jnp.int32)
    block = pl.BlockSpec((half, BLK, features), lambda i, _: (0, i, 0))
    vec = pl.BlockSpec((half, 32, features), lambda i, _: (0, tokens // 32, 0))
    own = pl.BlockSpec((half, span, features), lambda i, m: (0, m[0], 0))
    return pl.pallas_call(
        partial(norm_kernel, width=width),
        out_shape=(
            jax.ShapeDtypeStruct((tokens, width), BF16),
            jax.ShapeDtypeStruct((span, width), BF16),
            jax.ShapeDtypeStruct((8, width), F32),
        ),
        grid_spec=pltpu.PrefetchScalarGridSpec(
            num_scalar_prefetch=1,
            grid=(tokens // BLK,),
            in_specs=[block, block, vec, vec, own, own],
            out_specs=(
                pl.BlockSpec((BLK, width), lambda i, _: (i, 0)),
                pl.BlockSpec((span, width), lambda i, _: (0, 0)),
                pl.BlockSpec((8, width), lambda i, _: (0, 0)),
            ),
        ),
        name="norm_gathered",
    )(me, mine, theirs, mine, theirs, mine, theirs)


def stacked_heads(block, head_dim):
    count = block.shape[1] // head_dim
    return jnp.concatenate([block[:, h * head_dim : (h + 1) * head_dim] for h in range(count)], 0)


def dot_last(left, right):
    return lax.dot_general(left, right, (((1,), (1,)), ((), ())), preferred_element_type=F32)


def dot_first(left, right):
    return lax.dot_general(left, right, (((0,), (0,)), ((), ())), preferred_element_type=F32)


def dot_plain(left, right):
    return lax.dot_general(left, right, (((1,), (0,)), ((), ())), preferred_element_type=F32)


def key_pieces(kb, me, per_col, per_block, half):
    col = lax.div(kb, per_col)
    first = lax.rem(kb, per_col) * per_block
    places = []
    for t in range(per_block):
        apart = jnp.bitwise_xor(first + t, me)
        places.append((apart & 1) * half + lax.shift_right_logical(apart, 1))
    return col, places


def forward_kernel(
    low_ref, high_ref, me_ref, q_ref, kv_ref, bias_ref, out_ref, log_ref, low_out_ref, acc_ref, top_ref, sum_ref,
    *, head_dim, per_col, per_block, span
):
    chunk = pl.program_id(0)
    q = stacked_heads(q_ref[...], head_dim)
    rows = q.shape[0]
    acc_ref[...] = jnp.zeros_like(acc_ref)
    top_ref[...] = jnp.full_like(top_ref, NEGATIVE)
    sum_ref[...] = jnp.zeros_like(sum_ref)
    factor = head_dim ** (-0.5) * LOG2E

    def visit(kb, carry):
        col, places = key_pieces(kb, me_ref[0], per_col, per_block, kv_ref.shape[0] // 2)
        at = pl.ds(pl.multiple_of(col * span, span), span)
        kv = jnp.concatenate([kv_ref[place, at, :] for place in places], 0)
        scores = dot_last(kv[:, :head_dim], q) * factor
        old = top_ref[...]
        new = jnp.maximum(old, jnp.max(scores, 0, keepdims=True))
        weights = jnp.exp2(scores - new)
        decay = jnp.exp2(old - new)
        top_ref[...] = new
        sum_ref[...] = sum_ref[...] * decay + jnp.sum(weights, 0, keepdims=True)
        acc_ref[...] = acc_ref[...] * decay + dot_first(kv[:, head_dim:], weights.astype(BF16))
        return carry

    lax.fori_loop(low_ref[chunk], high_ref[chunk], visit, 0)
    out = acc_ref[...] / sum_ref[...]
    out_ref[0] = out
    for h in range(rows // BLK):
        low_out_ref[:, h * head_dim : (h + 1) * head_dim] = (
            jnp.transpose(out[:, h * BLK : (h + 1) * BLK]) + bias_ref[...]
        ).astype(BF16)
    log_ref[0] = top_ref[...] + jnp.log2(sum_ref[...])


def backward_kernel(
    low_ref, high_ref, me_ref, q_ref, grad_ref, out_ref, log_ref, kv_ref, gq_ref, gk_mine, gk_theirs, gv_mine, gv_theirs,
    gk_acc, gv_acc, gq_acc,
    *, head_dim, per_col, per_block, span
):
    chunk = pl.program_id(0)

    @pl.when(chunk == 0)
    def _():
        gk_acc[...] = jnp.zeros_like(gk_acc)
        gv_acc[...] = jnp.zeros_like(gv_acc)

    q = stacked_heads(q_ref[...], head_dim)
    grad = stacked_heads(grad_ref[...], head_dim)
    scale = head_dim ** (-0.5)
    log = log_ref[0]
    delta = jnp.sum(out_ref[0] * jnp.transpose(grad.astype(F32)), 0, keepdims=True)
    gq_acc[...] = jnp.zeros_like(gq_acc)

    def visit(kb, carry):
        col, places = key_pieces(kb, me_ref[0], per_col, per_block, kv_ref.shape[0] // 2)
        at = pl.ds(pl.multiple_of(col * span, span), span)
        kv = jnp.concatenate([kv_ref[place, at, :] for place in places], 0)
        keys, vals = kv[:, :head_dim], kv[:, head_dim:]
        scores = dot_last(keys, q) * (scale * LOG2E)
        probs = jnp.exp2(scores - log)
        grad_probs = dot_last(vals, grad)
        grad_scores = (probs * (grad_probs - delta)).astype(BF16)
        gq_acc[...] += dot_first(keys, grad_scores)
        gk = dot_plain(grad_scores, q)
        gv = dot_plain(probs.astype(BF16), grad)
        for t, place in enumerate(places):
            gk_acc[place, at, :] += gk[t * span : (t + 1) * span]
            gv_acc[place, at, :] += gv[t * span : (t + 1) * span]
        return carry

    lax.fori_loop(low_ref[chunk], high_ref[chunk], visit, 0)
    gq = gq_acc[...] * scale
    for h in range(q.shape[0] // BLK):
        gq_ref[:, h * head_dim : (h + 1) * head_dim] = jnp.transpose(
            gq[:, h * BLK : (h + 1) * BLK]
        ).astype(BF16)

    @pl.when(chunk == pl.num_programs(0) - 1)
    def _():
        half = gk_mine.shape[0]
        gk_mine[...] = gk_acc[:half] * scale
        gk_theirs[...] = (gk_acc[half:] * scale).astype(BF16)
        gv_mine[...] = gv_acc[:half]
        gv_theirs[...] = gv_acc[half:].astype(BF16)


def attention_calls(seq_blocks, tokens_col, span, head_dim, query_cols):
    rows, cols = lax.axis_size("row"), lax.axis_size("col")
    per_col, per_block = tokens_col // BLK, BLK // span
    heads = query_cols // head_dim
    me = lax.axis_index("row")
    ends = jnp.cumsum(seq_blocks)
    blocks = lax.axis_index("col") * per_col + jnp.arange(per_col, dtype=jnp.int32)
    owner = jnp.sum((blocks[:, None] >= ends[None, :]).astype(jnp.int32), 1)
    starts = ends - seq_blocks
    low = jnp.sum(
        jnp.where(owner[:, None] == jnp.arange(ends.shape[0])[None, :], starts[None, :], 0), 1
    ).astype(jnp.int32)
    scalars = (low, (blocks + 1).astype(jnp.int32), jnp.full((1,), me, jnp.int32))
    sizes = dict(head_dim=head_dim, per_col=per_col, per_block=per_block, span=span)
    chunk_rows = pl.BlockSpec((BLK, query_cols), lambda c, *_: (c, 0))
    whole_kv = pl.BlockSpec((rows, cols * span, 2 * head_dim), lambda c, *_: (0, 0, 0))
    half_kv = pl.BlockSpec((rows // 2, cols * span, head_dim), lambda c, *_: (0, 0, 0))
    turned = pl.BlockSpec((1, head_dim, heads * BLK), lambda c, *_: (c, 0, 0))
    logs = pl.BlockSpec((1, 1, heads * BLK), lambda c, *_: (c, 0, 0))
    bias = pl.BlockSpec((1, head_dim), lambda c, *_: (0, 0))
    shape = jax.ShapeDtypeStruct

    def forward(queries, key_values, bias_value):
        return pl.pallas_call(
            partial(forward_kernel, **sizes),
            out_shape=(
                shape((per_col, head_dim, heads * BLK), F32),
                shape((per_col, 1, heads * BLK), F32),
                shape((tokens_col, query_cols), BF16),
            ),
            grid_spec=pltpu.PrefetchScalarGridSpec(
                num_scalar_prefetch=3,
                grid=(per_col,),
                in_specs=[chunk_rows, whole_kv, bias],
                out_specs=(turned, logs, chunk_rows),
                scratch_shapes=[
                    pltpu.VMEM((head_dim, heads * BLK), F32),
                    pltpu.VMEM((1, heads * BLK), F32),
                    pltpu.VMEM((1, heads * BLK), F32),
                ],
            ),
            name="attend_forward",
        )(*scalars, queries, key_values, bias_value)

    def backward(queries, grad_low, out, log, key_values):
        return pl.pallas_call(
            partial(backward_kernel, **sizes),
            out_shape=(
                shape((tokens_col, query_cols), BF16),
                shape((rows // 2, cols * span, head_dim), F32),
                shape((rows // 2, cols * span, head_dim), BF16),
                shape((rows // 2, cols * span, head_dim), F32),
                shape((rows // 2, cols * span, head_dim), BF16),
            ),
            grid_spec=pltpu.PrefetchScalarGridSpec(
                num_scalar_prefetch=3,
                grid=(per_col,),
                in_specs=[chunk_rows, chunk_rows, turned, logs, whole_kv],
                out_specs=(chunk_rows, half_kv, half_kv, half_kv, half_kv),
                scratch_shapes=[
                    pltpu.VMEM((rows, cols * span, head_dim), F32),
                    pltpu.VMEM((rows, cols * span, head_dim), F32),
                    pltpu.VMEM((head_dim, heads * BLK), F32),
                ],
            ),
            name="attend_backward",
        )(*scalars, queries, grad_low, out, log, key_values)

    return forward, backward


def norm_forward(values):
    mean = jnp.mean(values, 1, keepdims=True)
    centred = values - mean
    scale = lax.rsqrt(jnp.mean(centred * centred, 1, keepdims=True) + EPSILON)
    return centred * scale, scale


def norm_backward(grad_out, normed, scale, gain):
    grad_normed = grad_out * gain
    plain = jnp.mean(grad_normed, 1, keepdims=True)
    cross = jnp.mean(grad_normed * normed, 1, keepdims=True)
    grad_in = scale * (grad_normed - plain - normed * cross)
    return grad_in, jnp.sum(grad_out * normed, 0), jnp.sum(grad_out, 0)


def body(
    inputs,
    cotangent,
    seq_blocks,
    first_gain,
    first_shift,
    w_query,
    b_query,
    w_keyval,
    b_value,
    w_out,
    b_out,
    second_gain,
    second_shift,
    w_up,
    b_up,
    w_down,
    b_down,
):
    rows, cols = lax.axis_size("row"), lax.axis_size("col")
    row, col = lax.axis_index("row"), lax.axis_index("col")
    tokens_col, features = inputs.shape
    width = features * rows
    span = tokens_col // rows
    head_dim = b_value.shape[0]
    kv_cols = w_keyval.shape[1]
    head_cols = w_query.shape[1]
    query_cols = head_cols * cols // rows
    heads_each = head_cols // query_cols

    up_cols = w_up.shape[1]

    vectors = jnp.stack([first_gain, first_shift, b_out, second_gain, second_shift, b_down])
    vectors = in_parts(padded(vectors, 8), 3).reshape(24, features)
    steps_x = row_gather(jnp.concatenate([inputs, padded(vectors, 32)], 0))
    fly_x = next(steps_x)
    kv_local = w_keyval.reshape(-1, query_cols)
    local_rows = kv_local.shape[0]
    bias_local = in_parts(b_query.reshape(heads_each, query_cols), 3).reshape(-1, query_cols)
    bias_rows = bias_local.shape[0]
    kv_local = jnp.concatenate([kv_local, padded(bias_local, 16)], 0)
    fly_kv = col_parts(kv_local)
    query_local = jnp.transpose(w_query.reshape(features, heads_each, query_cols), (1, 0, 2))
    fly_x, fly_kv, query_local, w_out_late = barrier(fly_x, fly_kv, query_local, w_out)

    fly_q = col_parts(query_local)
    fly_out = col_parts(w_out_late)
    fly_x = advance(steps_x, fly_x)
    kv_join = col_join(kv_local, fly_kv)
    kv_strip = jnp.transpose(
        kv_join[:, :local_rows].reshape(cols, features, kv_cols), (1, 0, 2)
    ).reshape(features, cols * kv_cols)
    bias_parts = lax.dynamic_index_in_dim(
        kv_join[:, local_rows : local_rows + bias_rows], row // heads_each, 0, keepdims=False
    ).reshape(3, heads_each, query_cols)
    bias_query = jnp.sum(
        lax.dynamic_index_in_dim(bias_parts, row % heads_each, 1, keepdims=True).astype(F32), 0
    )
    steps_kv = row_gather(kv_strip)
    fly_kv = next(steps_kv)
    fly_x, fly_kv, fly_q, w_up_late = barrier(fly_x, fly_kv, fly_q, w_up)

    w_up_all = lax.all_gather(w_up_late, "row", axis=0, tiled=True)
    query_flat = col_join(query_local, fly_q).reshape(rows, features, query_cols)
    w_query_row = exchange_rows(query_flat)
    fly_x = advance(steps_x, fly_x)
    fly_kv = advance(steps_kv, fly_kv)
    fly_x, fly_kv = barrier(fly_x, fly_kv)

    fly_kv = advance(steps_kv, fly_kv)
    mine, theirs = finish(steps_x, fly_x)
    first_all, own_low, vectors = norm_gathered(mine, theirs, tokens_col, span)
    gain1, shift1, bias_out, gain2, shift2, bias_down = (vectors[k : k + 1] for k in range(6))
    first_all, own_low, fly_kv, w_query_row, cot_late = barrier(
        first_all, own_low, fly_kv, w_query_row, cotangent
    )

    w_kv_all = in_row_order(jnp.concatenate(finish(steps_kv, fly_kv), 0), 0)
    own = own_low.astype(F32)
    first_low = lax.dynamic_slice_in_dim(first_all, row * span, span, 0)
    kv_own = dot_plain(first_low, w_kv_all).astype(BF16)
    fly_kv = col_parts(kv_own)
    cot_own = lax.all_to_all(cot_late, "row", 0, 1, tiled=True)
    fly_kv, fly_out, cot_own = barrier(fly_kv, fly_out, cot_own)
    w_out_all = lax.all_gather(
        col_join(w_out, fly_out).reshape(cols * head_cols, features), "row", axis=1, tiled=True
    )
    steps_kv = row_gather(col_join(kv_own, fly_kv).reshape(cols * span, -1))
    fly_kv = next(steps_kv)
    queries = (dot_plain(first_all, w_query_row.reshape(width, query_cols)) + bias_query).astype(
        BF16
    )
    kv_all = jnp.concatenate(finish(steps_kv, fly_kv), 0)
    queries, kv_all, w_up_all = barrier(queries, kv_all, w_up_all)
    fly_cot = col_parts(cot_own)
    w_down_late, _ = barrier(w_down, queries)
    w_down_all = lax.all_gather(w_down_late, "row", axis=1, tiled=True)

    attend, attend_back = attention_calls(seq_blocks, tokens_col, span, head_dim, query_cols)
    core_turned, logs, attn_low = attend(queries, kv_all, b_value[None, :])
    attn_own = lax.all_to_all(attn_low, "row", 0, 1, tiled=True)
    attn_own, w_out_all, fly_cot = barrier(attn_own, w_out_all, fly_cot)
    middle = own + dot_plain(attn_own, w_out_all) + bias_out

    normed2, scale2 = norm_forward(middle)
    second_low = (normed2 * gain2 + shift2).astype(BF16)
    fly_second = col_parts(second_low)
    query_strip = jnp.transpose(query_flat, (1, 0, 2)).reshape(features, rows * query_cols)
    query_strip, _ = barrier(query_strip, second_low)
    w_query_all = lax.all_gather(query_strip, "row", axis=0, tiled=True)
    cot_all = col_join(cot_own, fly_cot).reshape(cols * span, width)
    fly_second, cot_all = barrier(fly_second, cot_all)
    second_all = col_join(second_low, fly_second).reshape(cols * span, width)
    pre = dot_plain(second_all, w_up_all) + b_up
    grad_hidden = dot_last(cot_all, w_down_all)
    gelu_value, gelu_back = jax.vjp(partial(jax.nn.gelu, approximate=True), pre)
    hidden = gelu_value.astype(BF16)
    grad_pre = gelu_back(grad_hidden)[0].astype(BF16)
    second_part = dot_last(grad_pre, w_up_all).reshape(cols, span, width).astype(BF16)
    second_part, hidden, grad_pre = barrier(second_part, hidden, grad_pre)
    fly_second = col_send(second_part)
    hidden_late, _ = barrier(hidden, fly_second[1])
    up_part = dot_first(second_all, grad_pre).astype(BF16)
    down_part = dot_first(hidden, cot_all).astype(BF16)
    grad_w_down = lax.psum_scatter(down_part, "row", scatter_dimension=1, tiled=True).astype(F32)
    grad_w_up = lax.psum_scatter(up_part, "row", scatter_dimension=0, tiled=True).astype(F32)
    out_part = dot_plain(hidden_late, w_down_all).astype(BF16)
    up_sum = jnp.sum(grad_pre.astype(F32), 0)
    fly_second, _, _, out_part, up_sum = barrier(fly_second, down_part, up_part, out_part, up_sum)
    fly_block = col_send(out_part.reshape(cols, span, width))

    grad_in2, gain2_part, shift2_part = norm_backward(add_up(fly_second), normed2, scale2, gain2)
    grad_middle = cot_own.astype(F32) + grad_in2
    mid_low = grad_middle.astype(BF16)
    late = {}

    def hold(ready):
        if "grad_attn" in late:
            ready, late["grad_attn"] = barrier(ready, late["grad_attn"])
        return list(ready)

    steps_mid = row_gather(mid_low, hold)
    fly_mid = next(steps_mid)
    grad_attn_own = dot_last(mid_low, w_out_all).astype(BF16)
    fly_mid, grad_attn_own = barrier(fly_mid, grad_attn_own)
    late["grad_attn"] = lax.all_to_all(grad_attn_own, "row", 1, 0, tiled=True)
    fly_mid = advance(steps_mid, fly_mid)
    grad_attn = late.pop("grad_attn")

    grad_queries, key_mine, key_theirs, value_mine, value_theirs = attend_back(
        queries, grad_attn, core_turned, logs, kv_all
    )
    grad_queries, key_theirs, value_theirs, fly_mid, fly_block = barrier(
        grad_queries, key_theirs, value_theirs, fly_mid, fly_block
    )

    queries_own = lax.all_to_all(grad_queries, "row", 0, 1, tiled=True)
    steps_kv = row_scatter([key_mine, value_mine], [key_theirs, value_theirs])
    fly_kv = next(steps_kv)
    fly_mid = advance(steps_mid, fly_mid)
    query_part = dot_first(first_all, grad_queries).astype(BF16)
    query_bias = padded(in_parts(jnp.sum(grad_queries.astype(F32), 0), 2), 16)
    up_bias = in_parts(up_sum, 2).reshape(-1, query_cols)
    up_rows = up_bias.shape[0]
    extra = jnp.concatenate([query_bias, padded(up_bias, 16)], 0)
    attn_tokens = attn_low.reshape(rows, span, query_cols)
    apart = [2 * k for k in range(rows // 2)]

    def attn_rows(offset):
        return jnp.concatenate(
            [
                lax.dynamic_index_in_dim(attn_tokens, row ^ (p + offset), 0, keepdims=False)
                for p in apart
            ],
            0,
        )

    attn_mine, attn_theirs = attn_rows(0), attn_rows(1)
    fly_kv, fly_mid, queries_own, attn_mine, attn_theirs = barrier(
        fly_kv, fly_mid, queries_own, attn_mine, attn_theirs
    )
    out_own = (middle + add_up(fly_block) + bias_down).astype(BF16)
    fly_kv = advance(steps_kv, fly_kv)
    mid_mine, mid_theirs = finish(steps_mid, fly_mid)
    out_weights = (
        dot_first(mid_mine.reshape(-1, width), attn_mine)
        + dot_first(mid_theirs.reshape(-1, width), attn_theirs)
    ).astype(BF16)
    pieces = jnp.concatenate(
        [
            jnp.transpose(out_own.reshape(span, rows, features), (1, 0, 2)),
            out_weights.reshape(rows, features, query_cols),
            query_part.reshape(rows, features, query_cols),
            jnp.broadcast_to(extra[None], (rows,) + extra.shape),
        ],
        1,
    )
    kv_group = jnp.concatenate(finish(steps_kv, fly_kv), -1)

    pieces, kv_group, grad_attn_own = barrier(pieces, kv_group, grad_attn_own)
    fly_kv = col_send(kv_group.reshape(cols, span, -1))
    sent = exchange_rows(pieces)
    kv_mine = add_up(fly_kv).astype(BF16)
    grad_first = dot_last(queries_own, w_query_all) + dot_last(kv_mine, w_kv_all)
    normed1, scale1 = norm_forward(own)
    grad_in1, gain1_part, shift1_part = norm_backward(grad_first, normed1, scale1, gain1)
    feature_parts = jnp.stack(
        [
            gain1_part,
            shift1_part,
            gain2_part,
            shift2_part,
            jnp.sum(mid_low.astype(F32), 0),
            jnp.sum(cot_own.astype(F32), 0),
        ]
    )
    value_part = jnp.sum(grad_attn_own.astype(F32).reshape(-1, head_dim), 0)
    value_rows = jnp.tile(
        jnp.pad(in_parts(value_part, 2), ((0, 0), (0, features - head_dim))), (1, rows)
    )
    stacked = jnp.concatenate(
        [
            (grad_middle + grad_in1).astype(BF16),
            padded(jnp.concatenate([in_parts(feature_parts, 2).reshape(12, width), value_rows], 0), 16),
        ],
        0,
    )
    stacked, kv_mine, sent = barrier(stacked, kv_mine, sent)
    block_output = sent[:, :span].reshape(tokens_col, features)
    last_row = span + 2 * features + 16
    fly_weights = col_send(
        sent[:, span:last_row].reshape(cols, heads_each, 2 * features + 16, query_cols)
    )
    up_total = total(sent[:, last_row : last_row + up_rows]).reshape(2, up_cols)
    last = lax.all_to_all(stacked, "row", 1, 0, tiled=True).reshape(rows, -1, features)
    steps_kv = row_gather(kv_mine)
    kv_tokens = in_row_order(jnp.concatenate(finish(steps_kv, next(steps_kv)), 0), 0)
    first_mine = lax.dynamic_slice_in_dim(first_all, row * features, features, 1)
    kv_sum = dot_first(kv_tokens, first_mine).reshape(cols, kv_cols, features)
    last, kv_sum, grad_w_down, grad_w_up = barrier(last, kv_sum, grad_w_down, grad_w_up)
    grad_inputs = last[:, :span].reshape(tokens_col, features).astype(F32)
    sums = in_parts(total(last[:, -16:]), 2).reshape(32, features)
    fly_sums = col_send(
        jnp.concatenate(
            [kv_sum.astype(BF16), jnp.broadcast_to(sums[None], (cols, 32, features))], 1
        )
    )
    fly_weights, fly_sums = barrier(fly_weights, fly_sums)
    sums = add_up(fly_sums)
    grad_w_keyval = jnp.transpose(sums[:kv_cols])
    sums = sums[kv_cols : kv_cols + 16] + sums[kv_cols + 16 :]
    by_feature = sums[0:6] + sums[6:12]
    grad_b_value = (sums[12] + sums[13])[:head_dim]

    weights = add_up(fly_weights)
    grad_w_out = jnp.transpose(weights[:, :features], (0, 2, 1)).reshape(head_cols, features)
    grad_w_query = jnp.transpose(weights[:, features : 2 * features], (1, 0, 2)).reshape(
        features, head_cols
    )
    grad_b_query = (weights[:, 2 * features] + weights[:, 2 * features + 1]).reshape(head_cols)
    return (
        block_output,
        grad_inputs,
        by_feature[0],
        by_feature[1],
        grad_w_query,
        grad_b_query,
        grad_w_keyval,
        grad_b_value,
        grad_w_out,
        by_feature[4],
        by_feature[2],
        by_feature[3],
        grad_w_up,
        up_total[0] + up_total[1],
        grad_w_down,
        by_feature[5],
    )


def solution(mesh):
    both, rows, cols = P("col", "row"), P("row"), P("col")
    return jax.shard_map(
        body,
        mesh=mesh,
        in_specs=(
            both, both, P(), rows, rows, P("row", "col"), cols, P("row", "col"), P(), both, rows,
            rows, rows, P("row", "col"), cols, both, rows,
        ),
        out_specs=(
            both, both, rows, rows, P("row", "col"), cols, P("row", "col"), P(), both, rows,
            rows, rows, P("row", "col"), cols, both, rows,
        ),
        check_vma=False,
    )
```
